32 devices in a mesh: fsdp: 8 (over z, y), tp: 4 (over x, core).
Axes of the slice: x: 2, y: 2, z: 4, core: 2. Of those that a mesh axis runs over, the one named last changes fastest.
Arguments:
- grads: bfloat16 [8, 2, 4096, 2048], P('fsdp', None, 'tp'), may hold values from -144 to 144
- master: float32 [4096, 2048], P('tp', 'fsdp'), may hold values from -0.3125 to 0.3125
- moment: float32 [4096, 2048], P('tp', 'fsdp'), may hold values from -1.5 to 1.5
- second: float32 [4096, 2048], P('tp', 'fsdp'), may hold values from 0.02 to 0.3
- stats: float32 [4, 1024, 1024], P('tp', 'fsdp'), may hold values from -0.05 to 0.35
- basis: float32 [4, 1024, 1024], P('tp', 'fsdp'), may hold values from -0.5 to 1.5
Outputs:
- weights: bfloat16 [4096, 2048], P('tp')
- master_new: float32 [4096, 2048], P('tp', 'fsdp')
- moment_new: float32 [4096, 2048], P('tp', 'fsdp')
- second_new: float32 [4096, 2048], P('tp', 'fsdp')
- stats_new: float32 [4, 1024, 1024], P('tp', 'fsdp')
- basis_new: float32 [4, 1024, 1024], P('tp', 'fsdp')
The draws below stay inside these ranges and needn't reach their ends.
All inputs are finite; a program needn't handle non-finite values.
Results may differ from the reference program's by a relative error of at most 0.007.
Values may be sent and summed in bfloat16 or wider, within the bound.
A program may use at most 128 MiB of HBM per device.

```python
import math
import jax
import jax.numpy as jnp
from jax import lax

D = 4096
KVW = 2048
BS = 1024
MB = 2
NSK = 2
NBLK = 4
NREP = 8


def draw_grads(key, part):
    noise_key = jax.random.fold_in(key, 5)
    pair_key = jax.random.fold_in(key, 7)
    row_pos = jnp.arange(D).astype(jnp.float32) / float(D - 1)
    col_pos = jnp.arange(KVW).astype(jnp.float32) / float(KVW - 1)
    row_scale = jnp.exp(math.log(2.0) * row_pos)
    pairing = jax.random.permutation(pair_key, NREP)
    col_block = jnp.arange(KVW) // (KVW // NREP)
    spike = jnp.where(col_block[None, :] == pairing[:, None], 4.0, 1.0).astype(jnp.float32)
    noise = jnp.clip(jax.random.normal(noise_key, (NREP, MB, D, KVW), jnp.float32), -6.0, 6.0)
    col_scale = jnp.exp(math.log(3.0) * col_pos)
    return (noise * spike[:, None, None, :] * row_scale[None, None, :, None] * col_scale[None, None, None, :]).astype(jnp.bfloat16)


def draw_basis(key, part):
    identity = (jnp.arange(BS)[:, None] == jnp.arange(BS)[None, :]).astype(jnp.float32)
    noise = jax.random.normal(key, (NBLK, BS, BS), jnp.float32)
    return identity[None] + noise * (0.5 / math.sqrt(BS))


def draw_stats(key, part):
    identity = (jnp.arange(BS)[:, None] == jnp.arange(BS)[None, :]).astype(jnp.float32)
    first_key = jax.random.fold_in(key, 11)
    second_key = jax.random.fold_in(key, 23)
    levels = jax.random.uniform(first_key, (NBLK, BS), jnp.float32, math.log(0.02), math.log(0.2))
    noise = jax.random.normal(second_key, (NBLK, BS, BS), jnp.float32)
    symmetric = (noise + jnp.swapaxes(noise, 1, 2)) * (0.002 / math.sqrt(2.0))
    return identity[None] * jnp.exp(levels)[:, :, None] + symmetric * (1.0 - identity[None])


def shard_levels(rng, extent, pieces, least, top_value):
    factor_of, own = 1.0, jax.random.fold_in(rng, 6)
    for position, parts in pieces:
        steps = jnp.exp(jax.random.uniform(jax.random.fold_in(own, position), (parts,), jnp.float32, least / len(pieces), top_value / len(pieces)))
        factor_of = factor_of * jnp.repeat(steps, extent[position] // parts).reshape([-1 if axis == position else 1 for axis in range(len(extent))])
    return factor_of


def bell_draw(key, shape, scale, reach, shards=(), dtype=jnp.bfloat16):
    entries = scale * jax.random.normal(key, shape, jnp.float32)
    if shards:
        entries = entries * shard_levels(key, shape, shards, -0.22, 0.18)
    return jnp.clip(entries, -reach, reach).astype(dtype)


def setup_inputs(seed: int = 0) -> dict:
    keys = jax.random.split(jax.random.key(seed), 7)
    grads = draw_grads(jax.random.fold_in(keys[6], 71), 0)
    master = bell_draw(keys[1], (D, KVW), 0.02, 0.3125, ((0, 4), (1, 8)), jnp.float32)
    moment = bell_draw(keys[2], (D, KVW), 0.1, 1.5, ((0, 4), (1, 8)), jnp.float32)
    second = jnp.clip(jnp.exp(math.log(0.3) - 2.7080503 * jax.random.uniform(keys[3], (D, KVW), jnp.float32) ** shard_levels(keys[3], (D, KVW), ((0, 4), (1, 8)), -0.2, 0.2)), 0.02, 0.3)
    stats = draw_stats(jax.random.fold_in(keys[6], 71), 0)
    basis = draw_basis(jax.random.fold_in(keys[6], 71), 0)
    return dict(grads=grads, master=master, moment=moment, second=second, stats=stats, basis=basis)


poly_first = 3.4445
poly_second = -4.775
poly_third = 2.0315

def reference(grads, master, moment, second, stats, basis):
    high = lax.Precision.HIGHEST

    def accumulate(carry, replica):
        return (carry + lax.optimization_barrier(jnp.sum(replica.astype(jnp.float32), axis=0)), None)
    total, unused = lax.scan(accumulate, jnp.zeros((D, KVW), jnp.float32), grads)
    factor = jnp.minimum(1.0, jnp.sqrt(float(D * KVW) / (jnp.sum(total * total) + 1e-06)))
    clipped = (total * factor).reshape(NBLK, BS, KVW)
    rotated = jnp.einsum('bkr,bkc->brc', basis, clipped, precision=high).reshape(D, KVW)
    moment_new = 0.9 * moment + 0.1 * rotated
    second_new = 0.95 * second + 0.05 * rotated * rotated
    update = (moment_new / (jnp.sqrt(second_new) + 1e-08)).reshape(NBLK, BS, KVW)
    delta = jnp.einsum('brk,bkc->brc', basis, update, precision=high).reshape(D, KVW)
    master_new = master - 0.01 * (delta + 0.1 * master)
    weights = master_new.astype(jnp.bfloat16)
    outer = jnp.einsum('brc,bkc->brk', clipped, clipped, precision=high)
    stats_new = 0.9 * stats + 0.1 / KVW * outer
    power = jnp.einsum('brk,bkc->brc', stats_new, basis, precision=high)
    squares = lax.optimization_barrier(jnp.sum(power * power, axis=(1, 2), keepdims=True))
    current = power / jnp.sqrt(squares + 1e-06)
    for step in range(NSK):
        gram = jnp.einsum('bkr,bkc->brc', current, current, precision=high)
        product = jnp.einsum('brk,bkc->brc', current, gram, precision=high)
        second_term = jnp.einsum('brk,bkc->brc', product, gram, precision=high)
        current = poly_first * current + poly_second * product + poly_third * second_term
    return (weights, master_new, moment_new, second_new, stats_new, current)
```

```python
import functools

import jax
import jax.numpy as jnp
from jax import lax
from jax.experimental import pallas as pl
from jax.experimental.pallas import tpu as pltpu
from jax.sharding import PartitionSpec as P

D = 4096
KVW = 2048

poly_first = 3.4445
poly_second = -4.775
poly_third = 2.0315
bf16 = jnp.bfloat16
f32 = jnp.float32
MESH = pl.DeviceIdType.MESH
VMEM_BYTES = 40 * 1024 * 1024


def mm(a, b):
    return jnp.dot(a.astype(bf16), b.astype(bf16), preferred_element_type=f32)


def greet(n, tp_peers):
    me = lax.axis_index("fsdp")
    barrier = pltpu.get_barrier_semaphore()
    for step in range(1, n):
        pl.semaphore_signal(barrier, inc=1, device_id={"fsdp": lax.rem(me + step, n)}, device_id_type=MESH)
    if tp_peers > 1:
        lane = lax.axis_index("tp")
        for step in range(1, tp_peers):
            pl.semaphore_signal(barrier, inc=1, device_id={"tp": lax.rem(lane + step, tp_peers)}, device_id_type=MESH)
    pl.semaphore_wait(barrier, n - 1 + tp_peers - 1)


def remote(src, dst, send_sem, recv_sem, target, axis="fsdp"):
    return pltpu.make_async_remote_copy(
        src_ref=src, dst_ref=dst, send_sem=send_sem, recv_sem=recv_sem,
        device_id={axis: target}, device_id_type=MESH,
    )


def exchange(n, produce, finish, out1, in1, out2, in2, s1, r1, s2, r2, beside=None):
    half = n // 2
    me = lax.axis_index("fsdp")
    side = lax.rem(me, 2)
    pair = me // 2
    mate = me + 1 - 2 * side
    groups = [lax.rem(pair + 1 + k, half) for k in range(half)]
    first = [remote(out1.at[k], in1.at[k], s1.at[k], r1.at[k], mate) for k in range(half)]
    second = [remote(out2.at[k], in2.at[k], s2.at[k], r2.at[k], 2 * groups[k] + side) for k in range(half - 1)]

    def start(k):
        produce(2 * groups[k] + 1 - side, 2 * k, None, out1.at[k])
        first[k].start()

    for k in range(min(2, half)):
        start(k)
    for k in range(half):
        first[k].wait_recv()
        if k + 2 < half:
            start(k + 2)
        if k < half - 1:
            produce(2 * groups[k] + side, 2 * k + 1, in1.at[k], out2.at[k])
            second[k].start()
        if beside is not None:
            beside(k)
    for k in range(half - 1):
        second[k].wait_recv()
    finish(me, 2 * half - 1, in1.at[half - 1], in2)
    for k in range(half):
        first[k].wait_send()
    for k in range(half - 1):
        second[k].wait_send()


def outer_kernel(n, total, outer, out1, in1, out2, in2, s1, r1, s2, r2):
    half = n // 2
    strip = outer.shape[0]
    greet(n, 1)

    def local(chunk):
        at = pl.ds(pl.multiple_of(chunk * strip, strip), strip)
        return lax.dot_general(total[at, :], total[...], (((1,), (1,)), ((), ())), preferred_element_type=f32)

    def produce(chunk, slot, add, out):
        value = local(chunk)
        if add is not None:
            value = value + add[...].astype(f32)
        out[...] = value.astype(bf16)

    def finish(chunk, slot, add, others):
        value = local(chunk) + add[...].astype(f32)
        for k in range(half - 1):
            value = value + others[k].astype(f32)
        outer[...] = value

    exchange(n, produce, finish, out1, in1, out2, in2, s1, r1, s2, r2)


def sum_outer(total, n):
    rows = total.shape[0]
    strip = rows // n
    half = n // 2
    small = max(half - 1, 1)
    dma = pltpu.SemaphoreType.DMA
    piece = pltpu.VMEM((half, strip, rows), bf16)
    other = pltpu.VMEM((small, strip, rows), bf16)
    return pl.pallas_call(
        functools.partial(outer_kernel, n),
        out_shape=jax.ShapeDtypeStruct((strip, rows), f32),
        in_specs=[pl.BlockSpec(memory_space=pltpu.VMEM)],
        out_specs=pl.BlockSpec(memory_space=pltpu.VMEM),
        scratch_shapes=[piece, piece, other, other, dma((half,)), dma((half,)), dma((small,)), dma((small,))],
        compiler_params=pltpu.CompilerParams(collective_id=1, has_side_effects=True, vmem_limit_bytes=VMEM_BYTES),
    )(total)


def gather_kernel(n, own, every, s1, r1, s2, r2):
    half = n // 2
    me = lax.axis_index("fsdp")
    side = lax.rem(me, 2)
    pair = me // 2
    mate = me + 1 - 2 * side
    greet(n, 1)
    across = [remote(own, every.at[me], s2.at[k], r2.at[k], 2 * lax.rem(pair + 1 + k, half) + side)
              for k in range(half - 1)]
    for copy in across:
        copy.start()
    near = [remote(own, every.at[me], s1.at[0], r1.at[0], mate)]
    near[0].start()
    every[me] = own[...]
    for k in range(half - 1):
        across[k].wait_recv()
        source = 2 * lax.rem(pair + half - 1 - k, half) + side
        near.append(remote(every.at[source], every.at[source], s1.at[k + 1], r1.at[k + 1], mate))
        near[-1].start()
    for copy in near:
        copy.wait()
    for copy in across:
        copy.wait_send()


def gather_rows(own, n, key):
    strip, width = own.shape
    half = n // 2
    small = max(half - 1, 1)
    dma = pltpu.SemaphoreType.DMA
    every = pl.pallas_call(
        functools.partial(gather_kernel, n),
        out_shape=jax.ShapeDtypeStruct((n, strip, width), own.dtype),
        in_specs=[pl.BlockSpec(memory_space=pltpu.VMEM)],
        out_specs=pl.BlockSpec(memory_space=pltpu.VMEM),
        scratch_shapes=[dma((half,)), dma((half,)), dma((small,)), dma((small,))],
        compiler_params=pltpu.CompilerParams(collective_id=key, has_side_effects=True, vmem_limit_bytes=VMEM_BYTES),
    )(own)
    return every.reshape(n * strip, width)


MATE, NEAR, FAR = 1, 2, 4
LATE = (FAR, NEAR, MATE)
EARLY = (MATE, FAR, NEAR)
PARTS = 4
PLAN = (EARLY, LATE, EARLY, LATE)
HOPS = (FAR + NEAR, NEAR, FAR, 0)


def flip(device, mask):
    for bit in (MATE, NEAR, FAR):
        if mask & bit:
            device = device + bit - 2 * bit * lax.rem(device // bit, 2)
    return device


class Gather:
    def __init__(self, me, order, window, sends, recvs):
        self.me, self.order, self.window, self.sends, self.recvs = me, order, window, sends, recvs
        self.sent = []

    def copy(self, stage, sub):
        mask = sum(bit for i, bit in enumerate(self.order) if sub >> i & 1)
        place = self.window(flip(self.me, mask))
        index = 2 ** stage - 1 + sub
        return remote(place, place, self.sends.at[index], self.recvs.at[index], flip(self.me, self.order[stage]))

    def start(self, stage, sub):
        copy = self.copy(stage, sub)
        copy.start()
        self.sent.append(copy)

    def arrived(self, stage, sub):
        self.copy(stage, sub).wait_recv()

    def first(self):
        for stage in range(3):
            self.start(stage, 0)

    def second(self):
        self.arrived(0, 0)
        self.start(1, 1)
        self.start(2, 1)

    def third(self):
        self.arrived(1, 0)
        self.start(2, 2)

    def fourth(self):
        self.arrived(1, 1)
        self.start(2, 3)

    def last(self):
        for sub in range(4):
            self.arrived(2, sub)

    def close(self):
        for copy in self.sent:
            copy.wait_send()


def whole_kernel(n, lanes, grads, basis, stats, master, moment, second,
                 weights, master_new, moment_new, second_new, stats_new, refreshed,
                 held, out_y, in_y, out_z, in_z, whole, total, update, old_master, old_moment, old_second,
                 strip_y, got_y, strip_z, got_z, every, power, gram, gram_low, bend, once,
                 own_sq, in_sq, lane_sq, in_lane,
                 loads, y_s, y_r, z_s, z_r, q_s, q_r, sq_s, sq_r, lane_s, lane_r, b_s, b_r, p_s, p_r, w_s, w_r):
    rows, cols = total.shape
    strip = basis.shape[0]
    micro = held.shape[1]
    tile = 128
    piece = rows // 2
    me = lax.axis_index("fsdp")
    lane = lax.axis_index("tp")

    copies = []
    for k, mask in enumerate(HOPS):
        for which in (MATE, 0):
            start = pl.multiple_of(flip(me, mask + which) * cols, 128)
            slot = len(copies)
            copies.append(pltpu.make_async_copy(grads.at[0, :, :, pl.ds(start, cols)], held.at[slot], loads.at[slot]))
    states = [pltpu.make_async_copy(source, place, loads.at[n + i]) for i, (source, place) in enumerate(
        ((moment, old_moment), (second, old_second), (master, old_master)))]
    for i in (0, 1, 2, 3, 4, 5, 6, 7):
        copies[i].start()
    for copy in states:
        copy.start()
    greet(n, lanes)

    here = pl.ds(pl.multiple_of(me * strip, strip), strip)
    whole[here, :] = basis[...].astype(bf16)
    part_rows = strip // 2

    def basis_window(shift):
        def window(device):
            return whole.at[pl.ds(pl.multiple_of(device * strip + shift, part_rows), part_rows)]
        return window

    low = Gather(me, LATE, basis_window(0), b_s.at[0], b_r.at[0])
    top = Gather(me, EARLY, basis_window(part_rows), b_s.at[1], b_r.at[1])
    top.first()
    low.start(0, 0)
    low.start(1, 0)

    def local(slot, at):
        value = held[slot, 0, at, :].astype(f32)
        for index in range(1, micro):
            value = value + held[slot, index, at, :].astype(f32)
        return value

    def tiles(s, step, carry=0):
        def run(i, carry):
            return step(pl.ds(pl.multiple_of(s * piece + i * tile, tile), tile), carry)
        return lax.fori_loop(0, piece // tile, run, carry)

    def span(s):
        return pl.ds(s * piece, piece)

    y_copies = [remote(out_y.at[i // 2, span(i % 2)], in_y.at[i // 2, span(i % 2)], y_s.at[i], y_r.at[i], flip(me, MATE))
                for i in range(8)]
    z_copies = [remote(out_z.at[i // 2, span(i % 2)], in_z.at[i // 2, span(i % 2)], z_s.at[i], z_r.at[i],
                       flip(me, NEAR if i < 4 else FAR)) for i in range(6)]

    def start_y(i):
        k, s = divmod(i, 2)
        if s == 0:
            copies[2 * k].wait()

        def step(at, carry):
            out_y[k, at, :] = local(2 * k, at).astype(bf16)
            return carry

        tiles(s, step)
        y_copies[i].start()

    def start_z(k, s, extra):
        if s == 0:
            copies[2 * k + 1].wait()
        if extra is not None:
            z_copies[2 * extra + s].wait_recv()

        def step(at, carry):
            value = local(2 * k + 1, at) + in_y[k, at, :].astype(f32)
            if extra is not None:
                value = value + in_z[extra, at, :].astype(f32)
            out_z[k, at, :] = value.astype(bf16)
            return carry

        tiles(s, step)
        z_copies[2 * k + s].start()

    def close_total(s, carry):
        if s == 0:
            copies[7].wait()
        z_copies[2 + s].wait_recv()
        z_copies[4 + s].wait_recv()

        def step(at, carry):
            value = local(7, at) + in_y[3, at, :].astype(f32) + in_z[1, at, :].astype(f32) + in_z[2, at, :].astype(f32)
            total[at, :] = value.astype(bf16)
            return carry + jnp.sum((value * value).reshape(tile // 8, 8, cols), axis=0)

        return tiles(s, step, carry)

    start_y(0)
    start_y(1)
    sums = jnp.zeros((8, cols), f32)
    for i in range(8):
        k, s = divmod(i, 2)
        y_copies[i].wait_recv()
        if i + 2 < 8:
            start_y(i + 2)
        if k < 2:
            start_z(k, s, None)
        elif k == 2:
            start_z(k, s, 0)
        else:
            sums = close_total(s, sums)
        if i == 0:
            top.second()
            low.arrived(0, 0)
            low.start(1, 1)
        if i == 2:
            top.third()
        if i == 3:
            top.fourth()
        if i == 5:
            low.start(2, 0)
            low.start(2, 1)
            low.arrived(1, 0)
            low.start(2, 2)
            low.arrived(1, 1)
            low.start(2, 3)
    part = sums[:, :128]
    for c in range(1, cols // 128):
        part = part + sums[:, c * 128 : (c + 1) * 128]
    own_sq[...] = part
    sq_copies = [remote(own_sq, in_sq.at[k], sq_s.at[k], sq_r.at[k], lax.rem(me + 1 + k, n)) for k in range(n - 1)]
    for copy in sq_copies:
        copy.start()

    def product_strip(device):
        at = pl.ds(pl.multiple_of(device * strip, strip), strip)
        return lax.dot_general(total[at, :], total[...], (((1,), (1,)), ((), ())), preferred_element_type=f32)

    qy_copies = [remote(strip_y.at[k], got_y.at[k], q_s.at[k], q_r.at[k], flip(me, MATE)) for k in range(4)]
    qz_copies = [remote(strip_z.at[k], got_z.at[k], q_s.at[4 + k], q_r.at[4 + k], flip(me, FAR if k == 2 else NEAR))
                 for k in range(3)]

    def strip_start(k):
        strip_y[k] = product_strip(flip(me, HOPS[k] + MATE)).astype(bf16)
        qy_copies[k].start()

    def strip_pass(k):
        value = product_strip(flip(me, HOPS[k]))
        qy_copies[k].wait_recv()
        value = value + got_y[k].astype(f32)
        if k == 2:
            qz_copies[0].wait_recv()
            value = value + got_z[0].astype(f32)
        strip_z[k] = value.astype(bf16)
        qz_copies[k].start()

    strip_start(0)
    strip_start(1)
    value = own_sq[...]
    for k, copy in enumerate(sq_copies):
        copy.wait()
        value = value + in_sq[k]
    lane_sq[...] = value
    lane_copies = [remote(lane_sq, in_lane.at[k], lane_s.at[k], lane_r.at[k], lax.rem(lane + 1 + k, lanes), "tp")
                   for k in range(lanes - 1)]
    for copy in lane_copies:
        copy.start()
    strip_start(2)
    strip_start(3)
    for k, copy in enumerate(lane_copies):
        copy.wait()
        value = value + in_lane[k]
    squares = jnp.sum(value, keepdims=True)
    ratio = jnp.minimum(1.0, jnp.sqrt(float(D * KVW) / (squares + 1e-06)))
    strip_pass(0)

    top.last()
    low.last()
    for copy in states:
        copy.wait()
    part = rows // PARTS

    def rotate(i, carry):
        at = pl.ds(pl.multiple_of(i * part, part), part)
        rotated = lax.dot_general(whole[:, at], total[...], (((0,), (0,)), ((), ())), preferred_element_type=f32) * ratio
        first = 0.9 * old_moment[at, :] + 0.1 * rotated
        square = 0.95 * old_second[at, :] + 0.05 * rotated * rotated
        moment_new[at, :] = first
        second_new[at, :] = square
        update[at, :] = (first / (jnp.sqrt(square) + 1e-08)).astype(bf16)
        return carry

    lax.fori_loop(0, PARTS, rotate, 0)
    strip_pass(1)
    mine = pl.ds(pl.multiple_of(me * cols, 128), cols)

    def weight_window(i):
        def window(device):
            return weights.at[pl.ds(i * part, part), pl.ds(pl.multiple_of(device * cols, 128), cols)]
        return window

    out = [Gather(me, PLAN[i], weight_window(i), w_s.at[i], w_r.at[i]) for i in range(PARTS)]
    for i in range(PARTS):
        at = pl.ds(i * part, part)
        delta = jnp.dot(whole[at, :], update[...], preferred_element_type=f32)
        value = old_master[at, :]
        value = value - 0.01 * (delta + 0.1 * value)
        master_new[at, :] = value
        weights[at, mine] = value.astype(bf16)
        out[i].first()
        if i == 1:
            strip_pass(2)
    value = product_strip(me)
    qy_copies[3].wait_recv()
    qz_copies[1].wait_recv()
    value = value + got_y[3].astype(f32) + got_z[1].astype(f32)
    qz_copies[2].wait_recv()
    value = value + got_z[2].astype(f32)
    fresh = 0.9 * stats[...] + 0.1 / KVW * (value * (ratio * ratio))
    stats_new[...] = fresh
    coarse = fresh.astype(bf16)
    value = (jnp.dot(coarse, whole[...], preferred_element_type=f32)
             + jnp.dot((fresh - coarse.astype(f32)).astype(bf16), whole[...], preferred_element_type=f32))
    power[...] = value
    every[here, :] = value.astype(bf16)

    def power_window(device):
        return every.at[pl.ds(pl.multiple_of(device * strip, strip), strip)]

    spread = Gather(me, LATE, power_window, p_s, p_r)
    spread.first()
    out[0].second()
    spread.second()
    spread.third()
    out[1].second()
    spread.fourth()
    out[2].second()
    out[3].second()
    out[0].third()
    out[1].third()
    out[0].fourth()
    out[1].fourth()
    spread.last()

    def squares_of(i, carry):
        value = every[pl.ds(pl.multiple_of(i * 128, 128), 128), :].astype(f32)
        return carry + jnp.sum((value * value).reshape(16, 8, rows), axis=0)

    total_sq = jnp.sum(lax.fori_loop(0, rows // 128, squares_of, jnp.zeros((8, rows), f32)), keepdims=True)
    norm = 1.0 / jnp.sqrt(total_sq + 1e-06)
    block = 512

    def blocks(step):
        def run(i, carry):
            step(pl.ds(pl.multiple_of(i * block, block), block))
            return carry

        lax.fori_loop(0, rows // block, run, 0)

    def make_gram(at):
        value = lax.dot_general(every[:, at], every[...], (((0,), (0,)), ((), ())), preferred_element_type=f32)
        value = value * (norm * norm)
        gram[at, :] = value
        gram_low[at, :] = value.astype(bf16)

    def make_bend(at):
        value = poly_second * gram[at, :] + poly_third * mm(gram_low[at, :], gram_low[...])
        bend[at, :] = value.astype(bf16)

    def make_once(at):
        value = poly_first * gram[at, :] + mm(bend[at, :], gram_low[...])
        gram[at, :] = value
        once[at, :] = value.astype(bf16)

    def make_second(at):
        value = poly_first * gram[at, :] + mm(bend[at, :], once[...])
        gram_low[at, :] = value.astype(bf16)

    blocks(make_gram)
    out[2].third()
    out[3].third()
    blocks(make_bend)
    out[2].fourth()
    out[3].fourth()
    blocks(make_once)
    blocks(make_second)
    current = power[...] * norm
    current = poly_first * current + mm(current, bend[...])
    product = mm(current, gram_low[...])
    refreshed[...] = poly_first * current + poly_second * product + poly_third * mm(product, gram_low[...])
    for gather in out:
        gather.last()
    for copy in y_copies + z_copies + qy_copies + qz_copies:
        copy.wait_send()
    for gather in [top, low, spread] + out:
        gather.close()


def whole_step(grads, master, moment, second, stats, basis, n, lanes):
    unused, micro, rows, width = grads.shape
    cols = width // n
    strip = basis.shape[1]
    dma = pltpu.SemaphoreType.DMA
    vmem = pltpu.VMEM
    slab = (rows, cols)
    row = (strip, rows)
    low = vmem((rows, rows), bf16)
    small = vmem((8, 128), f32)
    others = max(lanes - 1, 1)
    block = pl.BlockSpec(memory_space=pltpu.VMEM)
    anywhere = pl.BlockSpec(memory_space=pl.ANY)
    f32_slab = jax.ShapeDtypeStruct(slab, f32)
    f32_row = jax.ShapeDtypeStruct(row, f32)
    outs = pl.pallas_call(
        functools.partial(whole_kernel, n, lanes),
        out_shape=(jax.ShapeDtypeStruct((rows, width), bf16), f32_slab, f32_slab, f32_slab, f32_row, f32_row),
        in_specs=[anywhere, block, block, anywhere, anywhere, anywhere],
        out_specs=(block,) * 6,
        scratch_shapes=[
            vmem((n, micro) + slab, bf16), vmem((4,) + slab, bf16), vmem((4,) + slab, bf16),
            vmem((3,) + slab, bf16), vmem((3,) + slab, bf16), low, vmem(slab, bf16), vmem(slab, bf16),
            vmem(slab, f32), vmem(slab, f32), vmem(slab, f32),
            vmem((4,) + row, bf16), vmem((4,) + row, bf16), vmem((3,) + row, bf16), vmem((3,) + row, bf16),
            low, vmem(row, f32), vmem((rows, rows), f32), low, low, low,
            small, vmem((n - 1, 8, 128), f32), small, vmem((others, 8, 128), f32),
            dma((n + 3,)), dma((8,)), dma((8,)), dma((6,)), dma((6,)), dma((7,)), dma((7,)),
            dma((n - 1,)), dma((n - 1,)), dma((others,)), dma((others,)),
            dma((2, 7)), dma((2, 7)), dma((7,)), dma((7,)), dma((PARTS, 7)), dma((PARTS, 7)),
        ],
        compiler_params=pltpu.CompilerParams(collective_id=0, has_side_effects=True, vmem_limit_bytes=60 * 1024 * 1024),
    )(grads, basis[0], stats[0], master, moment, second)
    weights, master_new, moment_new, second_new, stats_new, current = outs
    return (weights, master_new, moment_new, second_new, stats_new[None], current[None])


def plain_grads(grads, n, lanes):
    rows = grads.shape[2]
    local = jnp.sum(grads.astype(f32), axis=(0, 1)).astype(bf16)
    pieces = lax.all_to_all(local, "fsdp", split_axis=1, concat_axis=0, tiled=True)
    summed = jnp.sum(pieces.reshape(n, rows, -1).astype(f32), axis=0)
    squares = lax.psum(jnp.sum(summed * summed), ("fsdp", "tp"))
    return summed.astype(bf16), squares


def body(n, lanes, grads, master, moment, second, stats, basis):
    rows, cols = master.shape
    if n == 8 and cols % 128 == 0 and rows % (16 * PARTS) == 0 and basis.shape[1] % 32 == 0:
        return whole_step(grads, master, moment, second, stats, basis, n, lanes)
    own_rows = basis[0]
    stat_rows = stats[0]
    whole = lax.all_gather(own_rows.astype(bf16), "fsdp", axis=0, tiled=True)
    total, squares = plain_grads(grads, n, lanes)
    ratio = jnp.minimum(1.0, jnp.sqrt(float(D * KVW) / (squares + 1e-06)))
    rotated = mm(whole.T, total) * ratio
    moment_new = 0.9 * moment + 0.1 * rotated
    second_new = 0.95 * second + 0.05 * rotated * rotated
    update = moment_new / (jnp.sqrt(second_new) + 1e-08)
    delta = mm(whole, update)
    master_new = master - 0.01 * (delta + 0.1 * master)
    outer = sum_outer(total, n) * (ratio * ratio)
    stats_new = 0.9 * stat_rows + 0.1 / KVW * outer
    top = stats_new.astype(bf16)
    power = mm(top, whole) + mm(stats_new - top.astype(f32), whole)
    weights = lax.all_gather(master_new.astype(bf16), "fsdp", axis=1, tiled=True)
    every = gather_rows(power.astype(bf16), n, 2)
    raw = mm(every.T, every)
    norm = 1.0 / jnp.sqrt(jnp.sum(jnp.square(every.astype(f32))) + 1e-06)
    gram = raw * (norm * norm)
    current = power * norm
    bend = poly_second * gram + poly_third * mm(gram, gram)
    current = poly_first * current + mm(current, bend)
    once = poly_first * gram + mm(bend, gram)
    gram = poly_first * once + mm(bend, once)
    product = mm(current, gram)
    current = poly_first * current + poly_second * product + poly_third * mm(product, gram)
    return (weights, master_new, moment_new, second_new, stats_new[None], current[None])


def solution(mesh):
    in_specs = (
        P("fsdp", None, "tp", None),
        P("tp", "fsdp"),
        P("tp", "fsdp"),
        P("tp", "fsdp"),
        P("tp", "fsdp", None),
        P("tp", "fsdp", None),
    )
    out_specs = (
        P("tp", None),
        P("tp", "fsdp"),
        P("tp", "fsdp"),
        P("tp", "fsdp"),
        P("tp", "fsdp", None),
        P("tp", "fsdp", None),
    )
    step = functools.partial(body, mesh.shape["fsdp"], mesh.shape["tp"])
    return jax.shard_map(step, mesh=mesh, in_specs=in_specs, out_specs=out_specs, check_vma=False)
```

```python
import functools

import jax
import jax.numpy as jnp
from jax import lax
from jax.experimental import pallas as pl
from jax.experimental.pallas import tpu as pltpu
from jax.sharding import PartitionSpec as P

D = 4096
KVW = 2048

poly_first = 3.4445
poly_second = -4.775
poly_third = 2.0315
bf16 = jnp.bfloat16
f32 = jnp.float32
MESH = pl.DeviceIdType.MESH
VMEM_BYTES = 40 * 1024 * 1024


def mm(a, b):
    return jnp.dot(a.astype(bf16), b.astype(bf16), preferred_element_type=f32)


def greet(n, tp_peers):
    me = lax.axis_index("fsdp")
    barrier = pltpu.get_barrier_semaphore()
    for step in range(1, n):
        pl.semaphore_signal(barrier, inc=1, device_id={"fsdp": lax.rem(me + step, n)}, device_id_type=MESH)
    if tp_peers > 1:
        lane = lax.axis_index("tp")
        for step in range(1, tp_peers):
            pl.semaphore_signal(barrier, inc=1, device_id={"tp": lax.rem(lane + step, tp_peers)}, device_id_type=MESH)
    pl.semaphore_wait(barrier, n - 1 + tp_peers - 1)


def remote(src, dst, send_sem, recv_sem, target, axis="fsdp"):
    return pltpu.make_async_remote_copy(
        src_ref=src, dst_ref=dst, send_sem=send_sem, recv_sem=recv_sem,
        device_id={axis: target}, device_id_type=MESH,
    )


def exchange(n, produce, finish, out1, in1, out2, in2, s1, r1, s2, r2, beside=None):
    half = n // 2
    me = lax.axis_index("fsdp")
    side = lax.rem(me, 2)
    pair = me // 2
    mate = me + 1 - 2 * side
    groups = [lax.rem(pair + 1 + k, half) for k in range(half)]
    first = [remote(out1.at[k], in1.at[k], s1.at[k], r1.at[k], mate) for k in range(half)]
    second = [remote(out2.at[k], in2.at[k], s2.at[k], r2.at[k], 2 * groups[k] + side) for k in range(half - 1)]

    def start(k):
        produce(2 * groups[k] + 1 - side, 2 * k, None, out1.at[k])
        first[k].start()

    for k in range(min(2, half)):
        start(k)
    for k in range(half):
        first[k].wait_recv()
        if k + 2 < half:
            start(k + 2)
        if k < half - 1:
            produce(2 * groups[k] + side, 2 * k + 1, in1.at[k], out2.at[k])
            second[k].start()
        if beside is not None:
            beside(k)
    for k in range(half - 1):
        second[k].wait_recv()
    finish(me, 2 * half - 1, in1.at[half - 1], in2)
    for k in range(half):
        first[k].wait_send()
    for k in range(half - 1):
        second[k].wait_send()


def outer_kernel(n, total, outer, out1, in1, out2, in2, s1, r1, s2, r2):
    half = n // 2
    strip = outer.shape[0]
    greet(n, 1)

    def local(chunk):
        at = pl.ds(pl.multiple_of(chunk * strip, strip), strip)
        return lax.dot_general(total[at, :], total[...], (((1,), (1,)), ((), ())), preferred_element_type=f32)

    def produce(chunk, slot, add, out):
        value = local(chunk)
        if add is not None:
            value = value + add[...].astype(f32)
        out[...] = value.astype(bf16)

    def finish(chunk, slot, add, others):
        value = local(chunk) + add[...].astype(f32)
        for k in range(half - 1):
            value = value + others[k].astype(f32)
        outer[...] = value

    exchange(n, produce, finish, out1, in1, out2, in2, s1, r1, s2, r2)


def sum_outer(total, n):
    rows = total.shape[0]
    strip = rows // n
    half = n // 2
    small = max(half - 1, 1)
    dma = pltpu.SemaphoreType.DMA
    piece = pltpu.VMEM((half, strip, rows), bf16)
    other = pltpu.VMEM((small, strip, rows), bf16)
    return pl.pallas_call(
        functools.partial(outer_kernel, n),
        out_shape=jax.ShapeDtypeStruct((strip, rows), f32),
        in_specs=[pl.BlockSpec(memory_space=pltpu.VMEM)],
        out_specs=pl.BlockSpec(memory_space=pltpu.VMEM),
        scratch_shapes=[piece, piece, other, other, dma((half,)), dma((half,)), dma((small,)), dma((small,))],
        compiler_params=pltpu.CompilerParams(collective_id=1, has_side_effects=True, vmem_limit_bytes=VMEM_BYTES),
    )(total)


def gather_kernel(n, own, every, s1, r1, s2, r2):
    half = n // 2
    me = lax.axis_index("fsdp")
    side = lax.rem(me, 2)
    pair = me // 2
    mate = me + 1 - 2 * side
    greet(n, 1)
    across = [remote(own, every.at[me], s2.at[k], r2.at[k], 2 * lax.rem(pair + 1 + k, half) + side)
              for k in range(half - 1)]
    for copy in across:
        copy.start()
    near = [remote(own, every.at[me], s1.at[0], r1.at[0], mate)]
    near[0].start()
    every[me] = own[...]
    for k in range(half - 1):
        across[k].wait_recv()
        source = 2 * lax.rem(pair + half - 1 - k, half) + side
        near.append(remote(every.at[source], every.at[source], s1.at[k + 1], r1.at[k + 1], mate))
        near[-1].start()
    for copy in near:
        copy.wait()
    for copy in across:
        copy.wait_send()


def gather_rows(own, n, key):
    strip, width = own.shape
    half = n // 2
    small = max(half - 1, 1)
    dma = pltpu.SemaphoreType.DMA
    every = pl.pallas_call(
        functools.partial(gather_kernel, n),
        out_shape=jax.ShapeDtypeStruct((n, strip, width), own.dtype),
        in_specs=[pl.BlockSpec(memory_space=pltpu.VMEM)],
        out_specs=pl.BlockSpec(memory_space=pltpu.VMEM),
        scratch_shapes=[dma((half,)), dma((half,)), dma((small,)), dma((small,))],
        compiler_params=pltpu.CompilerParams(collective_id=key, has_side_effects=True, vmem_limit_bytes=VMEM_BYTES),
    )(own)
    return every.reshape(n * strip, width)


MATE, NEAR, FAR = 1, 2, 4
LATE = (FAR, NEAR, MATE)
EARLY = (MATE, FAR, NEAR)
PARTS = 4
READY = 2
VMEM_WHOLE = 41 * 1024 * 1024
PLAN = (EARLY, LATE, LATE, LATE)
HALF = 5
HOPS = (FAR + NEAR, NEAR, FAR, 0)


def flip(device, mask):
    for bit in (MATE, NEAR, FAR):
        if mask & bit:
            device = device + bit - 2 * bit * lax.rem(device // bit, 2)
    return device


class Gather:
    def __init__(self, me, order, window, sends, recvs):
        self.me, self.order, self.window, self.sends, self.recvs = me, order, window, sends, recvs
        self.sent = []

    def copy(self, stage, sub):
        mask = sum(bit for i, bit in enumerate(self.order) if sub >> i & 1)
        place = self.window(flip(self.me, mask))
        index = 2 ** stage - 1 + sub
        return remote(place, place, self.sends.at[index], self.recvs.at[index], flip(self.me, self.order[stage]))

    def start(self, stage, sub):
        copy = self.copy(stage, sub)
        copy.start()
        self.sent.append(copy)

    def arrived(self, stage, sub):
        self.copy(stage, sub).wait_recv()

    def mate(self):
        self.start(self.order.index(MATE), 0)

    def line(self):
        for bit in (FAR, NEAR):
            self.start(self.order.index(bit), 0)

    def first(self):
        for stage in range(3):
            self.start(stage, 0)

    def second(self):
        self.arrived(0, 0)
        self.start(1, 1)
        self.start(2, 1)

    def third(self):
        self.arrived(1, 0)
        self.start(2, 2)

    def fourth(self):
        self.arrived(1, 1)
        self.start(2, 3)

    def last(self):
        for sub in range(4):
            self.arrived(2, sub)

    def close(self):
        for copy in self.sent:
            copy.wait_send()


def whole_kernel(n, lanes, grads, basis, stats, master, moment, second,
                 weights, master_new, moment_new, second_new, stats_new, refreshed,
                 held, out_y, in_y, out_z, in_z, whole, total, update,
                 strip_y, got_y, strip_z, got_z, block_out, block_in, every, power, gram, gram_low, bend, once,
                 own_sq, in_sq, lane_sq, in_lane,
                 loads, y_s, y_r, z_s, z_r, q_s, q_r, sq_s, sq_r, lane_s, lane_r, b_s, b_r, p_s, p_r, w_s, w_r, x_s, x_r):
    rows, cols = moment_new.shape
    strip = stats.shape[0]
    wide = HALF * strip
    micro = held.shape[1]
    tile = 128
    piece = rows // 2
    me = lax.axis_index("fsdp")
    lane = lax.axis_index("tp")

    copies = []
    for k, mask in enumerate(HOPS):
        for which in (MATE, 0):
            start = pl.multiple_of(flip(me, mask + which) * cols, 128)
            slot = len(copies)
            copies.append(pltpu.make_async_copy(grads.at[0, :, :, pl.ds(start, cols)], held.at[slot], loads.at[slot]))
    states = [pltpu.make_async_copy(source, place, loads.at[n + i]) for i, (source, place) in enumerate(
        ((basis, refreshed), (moment, moment_new), (second, second_new), (master, master_new), (stats, stats_new)))]
    for copy in copies[:1] + states[:1] + copies[1:] + states[1:]:
        copy.start()
    greet(n, lanes)

    here = pl.ds(pl.multiple_of(me * strip, strip), strip)
    states[0].wait()
    whole[here, :] = refreshed[...].astype(bf16)
    part_rows = strip // 2

    def basis_window(shift):
        def window(device):
            return whole.at[pl.ds(pl.multiple_of(device * strip + shift, part_rows), part_rows)]
        return window

    low = Gather(me, LATE, basis_window(0), b_s.at[0], b_r.at[0])
    top = Gather(me, EARLY, basis_window(part_rows), b_s.at[1], b_r.at[1])
    top.first()
    low.start(0, 0)
    low.start(1, 0)

    def local(slot, at):
        value = held[slot, 0, at, :].astype(f32)
        for index in range(1, micro):
            value = value + held[slot, index, at, :].astype(f32)
        return value

    def tiles(s, step, carry=0):
        def run(i, carry):
            return step(pl.ds(pl.multiple_of(s * piece + i * tile, tile), tile), carry)
        return lax.fori_loop(0, piece // tile, run, carry)

    def span(s):
        return pl.ds(s * piece, piece)

    y_copies = [remote(out_y.at[i // 2, span(i % 2)], in_y.at[i // 2, span(i % 2)], y_s.at[i], y_r.at[i], flip(me, MATE))
                for i in range(8)]
    z_copies = [remote(out_z.at[i // 2, span(i % 2)], in_z.at[i // 2, span(i % 2)], z_s.at[i], z_r.at[i],
                       flip(me, NEAR if i < 4 else FAR)) for i in range(6)]

    def start_y(i):
        k, s = divmod(i, 2)
        if s == 0:
            copies[2 * k].wait()

        def step(at, carry):
            out_y[k, at, :] = local(2 * k, at).astype(bf16)
            return carry

        tiles(s, step)
        y_copies[i].start()

    def start_z(k, s, extra):
        if s == 0:
            copies[2 * k + 1].wait()
        if extra is not None:
            z_copies[2 * extra + s].wait_recv()

        def step(at, carry):
            value = local(2 * k + 1, at) + in_y[k, at, :].astype(f32)
            if extra is not None:
                value = value + in_z[extra, at, :].astype(f32)
            out_z[k, at, :] = value.astype(bf16)
            return carry

        tiles(s, step)
        z_copies[2 * k + s].start()

    def close_total(s, carry):
        if s == 0:
            copies[7].wait()
        z_copies[2 + s].wait_recv()
        z_copies[4 + s].wait_recv()

        def step(at, carry):
            value = local(7, at) + in_y[3, at, :].astype(f32) + in_z[1, at, :].astype(f32) + in_z[2, at, :].astype(f32)
            coarse = value.astype(bf16)
            total[at, :] = coarse
            if s == 0:
                total[pl.ds(pl.multiple_of(rows + at.start, tile), tile), :] = coarse
            return carry + jnp.sum((value * value).reshape(tile // 8, 8, cols), axis=0)

        return tiles(s, step, carry)

    def low_near():
        low.arrived(0, 0)
        low.start(1, 1)

    def low_mate():
        low.start(2, 0)
        low.start(2, 1)

    def low_rest():
        low.third()
        low.fourth()

    ahead = {6: [low_mate], 7: [low_rest]}
    after = {0: [top.second, low_near], 4: [top.third], 5: [top.fourth]}
    start_y(0)
    start_y(1)
    sums = jnp.zeros((8, cols), f32)
    for i in range(8):
        k, s = divmod(i, 2)
        y_copies[i].wait_recv()
        if i + 2 < 8:
            start_y(i + 2)
        for job in ahead.get(i, ()):
            job()
        if k < 2:
            start_z(k, s, None)
        elif k == 2:
            start_z(k, s, 0)
        else:
            sums = close_total(s, sums)
        for job in after.get(i, ()):
            job()
    part = sums[:, :128]
    for c in range(1, cols // 128):
        part = part + sums[:, c * 128 : (c + 1) * 128]
    own_sq[...] = part
    sq_copies = [remote(own_sq, in_sq.at[k], sq_s.at[k], sq_r.at[k], lax.rem(me + 1 + k, n)) for k in range(n - 1)]
    for copy in sq_copies:
        copy.start()

    def product_strip(device):
        at = pl.ds(pl.multiple_of(device * strip, strip), strip)
        right = pl.ds(pl.multiple_of(device * strip, strip), wide)
        return lax.dot_general(total[at, :], total[right, :], (((1,), (1,)), ((), ())), preferred_element_type=f32)

    qy_copies = [remote(strip_y.at[k], got_y.at[k], q_s.at[k], q_r.at[k], flip(me, MATE)) for k in range(4)]
    qz_copies = [remote(strip_z.at[k], got_z.at[k], q_s.at[4 + k], q_r.at[4 + k], flip(me, FAR if k == 2 else NEAR))
                 for k in range(3)]

    def strip_start(k):
        strip_y[k] = product_strip(flip(me, HOPS[k] + MATE)).astype(bf16)
        qy_copies[k].start()

    def strip_pass(k):
        value = product_strip(flip(me, HOPS[k]))
        qy_copies[k].wait_recv()
        value = value + got_y[k].astype(f32)
        if k == 2:
            qz_copies[0].wait_recv()
            value = value + got_z[0].astype(f32)
        strip_z[k] = value.astype(bf16)
        qz_copies[k].start()

    for k in range(4):
        strip_start(k)
    value = own_sq[...]
    for k, copy in enumerate(sq_copies):
        copy.wait()
        value = value + in_sq[k]
    lane_sq[...] = value
    lane_copies = [remote(lane_sq, in_lane.at[k], lane_s.at[k], lane_r.at[k], lax.rem(lane + 1 + k, lanes), "tp")
                   for k in range(lanes - 1)]
    for copy in lane_copies:
        copy.start()
    strip_pass(0)
    for k, copy in enumerate(lane_copies):
        copy.wait()
        value = value + in_lane[k]
    squares = jnp.sum(value, keepdims=True)
    ratio = jnp.minimum(1.0, jnp.sqrt(float(D * KVW) / (squares + 1e-06)))
    strip_pass(1)

    top.last()
    low.last()
    for copy in states[1:]:
        copy.wait()
    part = rows // PARTS

    def rotate(i, carry):
        at = pl.ds(pl.multiple_of(i * part, part), part)
        rotated = lax.dot_general(whole[:, at], total[:rows, :], (((0,), (0,)), ((), ())), preferred_element_type=f32) * ratio
        first = 0.9 * moment_new[at, :] + 0.1 * rotated
        square = 0.95 * second_new[at, :] + 0.05 * rotated * rotated
        moment_new[at, :] = first
        second_new[at, :] = square
        update[at, :] = (first / (jnp.sqrt(square) + 1e-08)).astype(bf16)
        return carry

    lax.fori_loop(0, PARTS, rotate, 0)
    strip_pass(2)
    def weight_window(i):
        def window(device):
            return weights.at[pl.ds(i * part, part), pl.ds(pl.multiple_of(device * cols, 128), cols)]
        return window

    mine = pl.ds(pl.multiple_of(me * cols, 128), cols)
    out = [Gather(me, PLAN[i], weight_window(i), w_s.at[i], w_r.at[i])
           for i in range(PARTS)]
    for i in range(PARTS):
        at = pl.ds(i * part, part)
        delta = jnp.dot(whole[at, :], update[...], preferred_element_type=f32)
        value = master_new[at, :]
        value = value - 0.01 * (delta + 0.1 * value)
        master_new[at, :] = value
        weights[at, mine] = value.astype(bf16)
        out[i].mate()
        if i < READY:
            out[i].line()
    value = product_strip(me)
    qy_copies[3].wait_recv()
    qz_copies[1].wait_recv()
    value = value + got_y[3].astype(f32) + got_z[1].astype(f32)
    qz_copies[2].wait_recv()
    value = value + got_z[2].astype(f32)
    crossing = []
    for k in range(1, HALF - 1):
        block_out[k - 1] = value[:, k * strip : (k + 1) * strip].astype(bf16)
        crossing.append(remote(block_out.at[k - 1], block_in.at[k - 1], x_s.at[k - 1], x_r.at[k - 1], lax.rem(me + k, n)))
        crossing[-1].start()

    def renew(offset, block):
        at = pl.ds(pl.multiple_of(lax.rem(me + offset, n) * strip, strip), strip)
        stats_new[:, at] = 0.9 * stats_new[:, at] + 0.1 / KVW * (block * (ratio * ratio))

    for k in range(HALF):
        renew(k, value[:, k * strip : (k + 1) * strip])
    for k in range(1, HALF - 1):
        crossing[k - 1].wait_recv()
        renew(n - k, block_in[k - 1].astype(f32).T)
    fresh = stats_new[...]
    coarse = fresh.astype(bf16)
    value = (jnp.dot(coarse, whole[...], preferred_element_type=f32)
             + jnp.dot((fresh - coarse.astype(f32)).astype(bf16), whole[...], preferred_element_type=f32))
    power[...] = value
    every[here, :] = value.astype(bf16)

    def power_window(device):
        return every.at[pl.ds(pl.multiple_of(device * strip, strip), strip)]

    spread = Gather(me, LATE, power_window, p_s, p_r)
    early = [gather for gather in out if gather.order == EARLY]
    late = [gather for gather in out if gather.order == LATE]
    spread.first()
    spread.second()
    spread.third()
    for gather in out[READY:]:
        gather.line()
    for gather in early:
        gather.second()
    spread.fourth()
    for gather in early:
        gather.third()
        gather.fourth()
    for gather in late:
        gather.second()
    spread.last()
    for gather in late:
        gather.third()

    def squares_of(i, carry):
        value = every[pl.ds(pl.multiple_of(i * 128, 128), 128), :].astype(f32)
        return carry + jnp.sum((value * value).reshape(16, 8, rows), axis=0)

    total_sq = jnp.sum(lax.fori_loop(0, rows // 128, squares_of, jnp.zeros((8, rows), f32)), keepdims=True)
    norm = 1.0 / jnp.sqrt(total_sq + 1e-06)
    block = 512

    def blocks(step):
        def run(i, carry):
            step(pl.ds(pl.multiple_of(i * block, block), block))
            return carry

        lax.fori_loop(0, rows // block, run, 0)

    def make_gram(at):
        value = lax.dot_general(every[:, at], every[...], (((0,), (0,)), ((), ())), preferred_element_type=f32)
        value = value * (norm * norm)
        gram[at, :] = value
        gram_low[at, :] = value.astype(bf16)

    def make_bend(at):
        value = poly_second * gram[at, :] + poly_third * mm(gram_low[at, :], gram_low[...])
        bend[at, :] = value.astype(bf16)

    def make_once(at):
        value = poly_first * gram[at, :] + mm(bend[at, :], gram_low[...])
        gram[at, :] = value
        once[at, :] = value.astype(bf16)

    def make_second(at):
        value = poly_first * gram[at, :] + mm(bend[at, :], once[...])
        gram_low[at, :] = value.astype(bf16)

    blocks(make_gram)
    for gather in late:
        gather.fourth()
    blocks(make_bend)
    blocks(make_once)
    blocks(make_second)
    current = power[...] * norm
    current = poly_first * current + mm(current, bend[...])
    product = mm(current, gram_low[...])
    refreshed[...] = poly_first * current + poly_second * product + poly_third * mm(product, gram_low[...])
    for gather in out:
        gather.last()
    for copy in y_copies + z_copies + qy_copies + qz_copies + crossing:
        copy.wait_send()
    for gather in [top, low, spread] + out:
        gather.close()


def hand_over(*refs):
    count = len(refs) // 2
    copies = [pltpu.make_async_copy(refs[i], refs[count + i], refs[-1].at[i]) for i in range(count)]
    for copy in copies:
        copy.start()
    for copy in copies:
        copy.wait()


def whole_step(grads, master, moment, second, stats, basis, n, lanes):
    unused, micro, rows, width = grads.shape
    cols = width // n
    strip = basis.shape[1]
    dma = pltpu.SemaphoreType.DMA
    vmem = pltpu.VMEM
    slab = (rows, cols)
    row = (strip, rows)
    part = (strip, HALF * strip)
    low = vmem((rows, rows), bf16)
    small = vmem((8, 128), f32)
    others = max(lanes - 1, 1)
    block = pl.BlockSpec(memory_space=pltpu.VMEM)
    far_block = pl.BlockSpec(memory_space=pltpu.HBM)
    f32_slab = jax.ShapeDtypeStruct(slab, f32)
    f32_row = jax.ShapeDtypeStruct(row, f32)
    outs = pl.pallas_call(
        functools.partial(whole_kernel, n, lanes),
        out_shape=(jax.ShapeDtypeStruct((rows, width), bf16), f32_slab, f32_slab, f32_slab, f32_row, f32_row),
        in_specs=[far_block] * 6,
        out_specs=(block,) * 6,
        scratch_shapes=[
            vmem((n, micro) + slab, bf16), vmem((4,) + slab, bf16), vmem((4,) + slab, bf16),
            vmem((3,) + slab, bf16), vmem((3,) + slab, bf16), low, vmem((rows + rows // 2, cols), bf16), vmem(slab, bf16),
            vmem((4,) + part, bf16), vmem((4,) + part, bf16), vmem((3,) + part, bf16), vmem((3,) + part, bf16),
            vmem((HALF - 2, strip, strip), bf16), vmem((HALF - 2, strip, strip), bf16),
            low, vmem(row, f32), vmem((rows, rows), f32), low, low, low,
            small, vmem((n - 1, 8, 128), f32), small, vmem((others, 8, 128), f32),
            dma((n + 5,)), dma((8,)), dma((8,)), dma((6,)), dma((6,)), dma((7,)), dma((7,)),
            dma((n - 1,)), dma((n - 1,)), dma((others,)), dma((others,)),
            dma((2, 7)), dma((2, 7)), dma((7,)), dma((7,)), dma((PARTS, 7)), dma((PARTS, 7)), dma((HALF - 2,)), dma((HALF - 2,)),
        ],
        compiler_params=pltpu.CompilerParams(collective_id=0, has_side_effects=True, vmem_limit_bytes=VMEM_WHOLE),
    )(*(pltpu.with_memory_space_constraint(value, pltpu.HBM) for value in (
        grads, basis[0], stats[0], master, moment, second)))
    weights, master_new, moment_new, second_new, stats_new, current = pl.pallas_call(
        hand_over,
        out_shape=tuple(jax.ShapeDtypeStruct(value.shape, value.dtype) for value in outs),
        in_specs=[block] * len(outs),
        out_specs=(far_block,) * len(outs),
        scratch_shapes=[dma((len(outs),))],
        compiler_params=pltpu.CompilerParams(vmem_limit_bytes=16 * 1024 * 1024),
    )(*outs)
    return (weights, master_new, moment_new, second_new, stats_new[None], current[None])


def plain_grads(grads, n, lanes):
    rows = grads.shape[2]
    local = jnp.sum(grads.astype(f32), axis=(0, 1)).astype(bf16)
    pieces = lax.all_to_all(local, "fsdp", split_axis=1, concat_axis=0, tiled=True)
    summed = jnp.sum(pieces.reshape(n, rows, -1).astype(f32), axis=0)
    squares = lax.psum(jnp.sum(summed * summed), ("fsdp", "tp"))
    return summed.astype(bf16), squares


def body(n, lanes, grads, master, moment, second, stats, basis):
    rows, cols = master.shape
    if n == 8 and cols % 128 == 0 and rows % (16 * PARTS) == 0 and basis.shape[1] % 128 == 0:
        return whole_step(grads, master, moment, second, stats, basis, n, lanes)
    own_rows = basis[0]
    stat_rows = stats[0]
    whole = lax.all_gather(own_rows.astype(bf16), "fsdp", axis=0, tiled=True)
    total, squares = plain_grads(grads, n, lanes)
    ratio = jnp.minimum(1.0, jnp.sqrt(float(D * KVW) / (squares + 1e-06)))
    rotated = mm(whole.T, total) * ratio
    moment_new = 0.9 * moment + 0.1 * rotated
    second_new = 0.95 * second + 0.05 * rotated * rotated
    update = moment_new / (jnp.sqrt(second_new) + 1e-08)
    delta = mm(whole, update)
    master_new = master - 0.01 * (delta + 0.1 * master)
    outer = sum_outer(total, n) * (ratio * ratio)
    stats_new = 0.9 * stat_rows + 0.1 / KVW * outer
    top = stats_new.astype(bf16)
    power = mm(top, whole) + mm(stats_new - top.astype(f32), whole)
    weights = lax.all_gather(master_new.astype(bf16), "fsdp", axis=1, tiled=True)
    every = gather_rows(power.astype(bf16), n, 2)
    raw = mm(every.T, every)
    norm = 1.0 / jnp.sqrt(jnp.sum(jnp.square(every.astype(f32))) + 1e-06)
    gram = raw * (norm * norm)
    current = power * norm
    bend = poly_second * gram + poly_third * mm(gram, gram)
    current = poly_first * current + mm(current, bend)
    once = poly_first * gram + mm(bend, gram)
    gram = poly_first * once + mm(bend, once)
    product = mm(current, gram)
    current = poly_first * current + poly_second * product + poly_third * mm(product, gram)
    return (weights, master_new, moment_new, second_new, stats_new[None], current[None])


def solution(mesh):
    in_specs = (
        P("fsdp", None, "tp", None),
        P("tp", "fsdp"),
        P("tp", "fsdp"),
        P("tp", "fsdp"),
        P("tp", "fsdp", None),
        P("tp", "fsdp", None),
    )
    out_specs = (
        P("tp", None),
        P("tp", "fsdp"),
        P("tp", "fsdp"),
        P("tp", "fsdp"),
        P("tp", "fsdp", None),
        P("tp", "fsdp", None),
    )
    step = functools.partial(body, mesh.shape["fsdp"], mesh.shape["tp"])
    return jax.shard_map(step, mesh=mesh, in_specs=in_specs, out_specs=out_specs, check_vma=False)
```

```python
import functools

import jax
import jax.numpy as jnp
from jax import lax
from jax.experimental import pallas as pl
from jax.experimental.pallas import tpu as pltpu
from jax.sharding import PartitionSpec as P

D = 4096
KVW = 2048

poly_first = 3.4445
poly_second = -4.775
poly_third = 2.0315
bf16 = jnp.bfloat16
f32 = jnp.float32
MESH = pl.DeviceIdType.MESH
VMEM_BYTES = 40 * 1024 * 1024


def mm(a, b):
    return jnp.dot(a.astype(bf16), b.astype(bf16), preferred_element_type=f32)


def greet(n, tp_peers):
    me = lax.axis_index("fsdp")
    barrier = pltpu.get_barrier_semaphore()
    for step in range(1, n):
        pl.semaphore_signal(barrier, inc=1, device_id={"fsdp": lax.rem(me + step, n)}, device_id_type=MESH)
    if tp_peers > 1:
        lane = lax.axis_index("tp")
        for step in range(1, tp_peers):
            pl.semaphore_signal(barrier, inc=1, device_id={"tp": lax.rem(lane + step, tp_peers)}, device_id_type=MESH)
    pl.semaphore_wait(barrier, n - 1 + tp_peers - 1)


def remote(src, dst, send_sem, recv_sem, target, axis="fsdp"):
    return pltpu.make_async_remote_copy(
        src_ref=src, dst_ref=dst, send_sem=send_sem, recv_sem=recv_sem,
        device_id={axis: target}, device_id_type=MESH,
    )


def exchange(n, produce, finish, out1, in1, out2, in2, s1, r1, s2, r2, beside=None):
    half = n // 2
    me = lax.axis_index("fsdp")
    side = lax.rem(me, 2)
    pair = me // 2
    mate = me + 1 - 2 * side
    groups = [lax.rem(pair + 1 + k, half) for k in range(half)]
    first = [remote(out1.at[k], in1.at[k], s1.at[k], r1.at[k], mate) for k in range(half)]
    second = [remote(out2.at[k], in2.at[k], s2.at[k], r2.at[k], 2 * groups[k] + side) for k in range(half - 1)]

    def start(k):
        produce(2 * groups[k] + 1 - side, 2 * k, None, out1.at[k])
        first[k].start()

    for k in range(min(2, half)):
        start(k)
    for k in range(half):
        first[k].wait_recv()
        if k + 2 < half:
            start(k + 2)
        if k < half - 1:
            produce(2 * groups[k] + side, 2 * k + 1, in1.at[k], out2.at[k])
            second[k].start()
        if beside is not None:
            beside(k)
    for k in range(half - 1):
        second[k].wait_recv()
    finish(me, 2 * half - 1, in1.at[half - 1], in2)
    for k in range(half):
        first[k].wait_send()
    for k in range(half - 1):
        second[k].wait_send()


def outer_kernel(n, total, outer, out1, in1, out2, in2, s1, r1, s2, r2):
    half = n // 2
    strip = outer.shape[0]
    greet(n, 1)

    def local(chunk):
        at = pl.ds(pl.multiple_of(chunk * strip, strip), strip)
        return lax.dot_general(total[at, :], total[...], (((1,), (1,)), ((), ())), preferred_element_type=f32)

    def produce(chunk, slot, add, out):
        value = local(chunk)
        if add is not None:
            value = value + add[...].astype(f32)
        out[...] = value.astype(bf16)

    def finish(chunk, slot, add, others):
        value = local(chunk) + add[...].astype(f32)
        for k in range(half - 1):
            value = value + others[k].astype(f32)
        outer[...] = value

    exchange(n, produce, finish, out1, in1, out2, in2, s1, r1, s2, r2)


def sum_outer(total, n):
    rows = total.shape[0]
    strip = rows // n
    half = n // 2
    small = max(half - 1, 1)
    dma = pltpu.SemaphoreType.DMA
    piece = pltpu.VMEM((half, strip, rows), bf16)
    other = pltpu.VMEM((small, strip, rows), bf16)
    return pl.pallas_call(
        functools.partial(outer_kernel, n),
        out_shape=jax.ShapeDtypeStruct((strip, rows), f32),
        in_specs=[pl.BlockSpec(memory_space=pltpu.VMEM)],
        out_specs=pl.BlockSpec(memory_space=pltpu.VMEM),
        scratch_shapes=[piece, piece, other, other, dma((half,)), dma((half,)), dma((small,)), dma((small,))],
        compiler_params=pltpu.CompilerParams(collective_id=1, has_side_effects=True, vmem_limit_bytes=VMEM_BYTES),
    )(total)


def gather_kernel(n, own, every, s1, r1, s2, r2):
    half = n // 2
    me = lax.axis_index("fsdp")
    side = lax.rem(me, 2)
    pair = me // 2
    mate = me + 1 - 2 * side
    greet(n, 1)
    across = [remote(own, every.at[me], s2.at[k], r2.at[k], 2 * lax.rem(pair + 1 + k, half) + side)
              for k in range(half - 1)]
    for copy in across:
        copy.start()
    near = [remote(own, every.at[me], s1.at[0], r1.at[0], mate)]
    near[0].start()
    every[me] = own[...]
    for k in range(half - 1):
        across[k].wait_recv()
        source = 2 * lax.rem(pair + half - 1 - k, half) + side
        near.append(remote(every.at[source], every.at[source], s1.at[k + 1], r1.at[k + 1], mate))
        near[-1].start()
    for copy in near:
        copy.wait()
    for copy in across:
        copy.wait_send()


def gather_rows(own, n, key):
    strip, width = own.shape
    half = n // 2
    small = max(half - 1, 1)
    dma = pltpu.SemaphoreType.DMA
    every = pl.pallas_call(
        functools.partial(gather_kernel, n),
        out_shape=jax.ShapeDtypeStruct((n, strip, width), own.dtype),
        in_specs=[pl.BlockSpec(memory_space=pltpu.VMEM)],
        out_specs=pl.BlockSpec(memory_space=pltpu.VMEM),
        scratch_shapes=[dma((half,)), dma((half,)), dma((small,)), dma((small,))],
        compiler_params=pltpu.CompilerParams(collective_id=key, has_side_effects=True, vmem_limit_bytes=VMEM_BYTES),
    )(own)
    return every.reshape(n * strip, width)


MATE, NEAR, FAR = 1, 2, 4
LATE = (FAR, NEAR, MATE)
EARLY = (MATE, FAR, NEAR)
PARTS = 4
READY = 1
VMEM_WHOLE = 41 * 1024 * 1024
PLAN = (EARLY, LATE, LATE, LATE)
HALF = 5
HOPS = (FAR + NEAR, NEAR, FAR, 0)


def flip(device, mask):
    for bit in (MATE, NEAR, FAR):
        if mask & bit:
            device = device + bit - 2 * bit * lax.rem(device // bit, 2)
    return device


class Gather:
    def __init__(self, me, order, window, sends, recvs):
        self.me, self.order, self.window, self.sends, self.recvs = me, order, window, sends, recvs
        self.sent = []

    def copy(self, stage, sub):
        mask = sum(bit for i, bit in enumerate(self.order) if sub >> i & 1)
        place = self.window(flip(self.me, mask))
        index = 2 ** stage - 1 + sub
        return remote(place, place, self.sends.at[index], self.recvs.at[index], flip(self.me, self.order[stage]))

    def start(self, stage, sub):
        copy = self.copy(stage, sub)
        copy.start()
        self.sent.append(copy)

    def arrived(self, stage, sub):
        self.copy(stage, sub).wait_recv()

    def mate(self):
        self.start(self.order.index(MATE), 0)

    def line(self):
        for bit in (FAR, NEAR):
            self.start(self.order.index(bit), 0)

    def first(self):
        for stage in range(3):
            self.start(stage, 0)

    def second(self):
        self.arrived(0, 0)
        self.start(1, 1)
        self.start(2, 1)

    def third(self):
        self.arrived(1, 0)
        self.start(2, 2)

    def fourth(self):
        self.arrived(1, 1)
        self.start(2, 3)

    def last(self):
        for sub in range(4):
            self.arrived(2, sub)

    def close(self):
        for copy in self.sent:
            copy.wait_send()


def whole_kernel(n, lanes, grads, basis, stats, master, moment, second,
                 weights, master_new, moment_new, second_new, stats_new, refreshed,
                 held, out_y, in_y, out_z, in_z, whole, total, update,
                 strip_y, got_y, strip_z, got_z, block_out, block_in, every, power, gram, gram_low, bend, once,
                 own_sq, in_sq, lane_sq, in_lane,
                 loads, y_s, y_r, z_s, z_r, q_s, q_r, sq_s, sq_r, lane_s, lane_r, b_s, b_r, p_s, p_r, w_s, w_r, x_s, x_r):
    rows, cols = moment_new.shape
    strip = stats.shape[0]
    wide = HALF * strip
    micro = held.shape[1]
    tile = 128
    piece = rows // 2
    me = lax.axis_index("fsdp")
    lane = lax.axis_index("tp")

    copies = []
    for k, mask in enumerate(HOPS):
        for which in (MATE, 0):
            start = pl.multiple_of(flip(me, mask + which) * cols, 128)
            slot = len(copies)
            copies.append(pltpu.make_async_copy(grads.at[0, :, :, pl.ds(start, cols)], held.at[slot], loads.at[slot]))
    states = [pltpu.make_async_copy(source, place, loads.at[n + i]) for i, (source, place) in enumerate(
        ((basis, refreshed), (moment, moment_new), (second, second_new), (master, master_new), (stats, stats_new)))]
    for copy in copies[:1] + states[:1] + copies[1:] + states[1:]:
        copy.start()
    greet(n, lanes)

    here = pl.ds(pl.multiple_of(me * strip, strip), strip)
    states[0].wait()
    whole[here, :] = refreshed[...].astype(bf16)
    part_rows = strip // 2

    def basis_window(shift):
        def window(device):
            return whole.at[pl.ds(pl.multiple_of(device * strip + shift, part_rows), part_rows)]
        return window

    low = Gather(me, LATE, basis_window(0), b_s.at[0], b_r.at[0])
    top = Gather(me, EARLY, basis_window(part_rows), b_s.at[1], b_r.at[1])
    top.first()
    low.start(0, 0)
    low.start(1, 0)

    def local(slot, at):
        value = held[slot, 0, at, :].astype(f32)
        for index in range(1, micro):
            value = value + held[slot, index, at, :].astype(f32)
        return value

    def tiles(s, step, carry=0):
        def run(i, carry):
            return step(pl.ds(pl.multiple_of(s * piece + i * tile, tile), tile), carry)
        return lax.fori_loop(0, piece // tile, run, carry)

    def span(s):
        return pl.ds(s * piece, piece)

    y_copies = [remote(out_y.at[i // 2, span(i % 2)], in_y.at[i // 2, span(i % 2)], y_s.at[i], y_r.at[i], flip(me, MATE))
                for i in range(8)]
    z_copies = [remote(out_z.at[i // 2, span(i % 2)], in_z.at[i // 2, span(i % 2)], z_s.at[i], z_r.at[i],
                       flip(me, NEAR if i < 4 else FAR)) for i in range(6)]

    def start_y(i):
        k, s = divmod(i, 2)
        if s == 0:
            copies[2 * k].wait()

        def step(at, carry):
            out_y[k, at, :] = local(2 * k, at).astype(bf16)
            return carry

        tiles(s, step)
        y_copies[i].start()

    def start_z(k, s, extra):
        if s == 0:
            copies[2 * k + 1].wait()
        if extra is not None:
            z_copies[2 * extra + s].wait_recv()

        def step(at, carry):
            value = local(2 * k + 1, at) + in_y[k, at, :].astype(f32)
            if extra is not None:
                value = value + in_z[extra, at, :].astype(f32)
            out_z[k, at, :] = value.astype(bf16)
            return carry

        tiles(s, step)
        z_copies[2 * k + s].start()

    def close_total(s, carry):
        if s == 0:
            copies[7].wait()
        z_copies[2 + s].wait_recv()
        z_copies[4 + s].wait_recv()

        def step(at, carry):
            value = local(7, at) + in_y[3, at, :].astype(f32) + in_z[1, at, :].astype(f32) + in_z[2, at, :].astype(f32)
            coarse = value.astype(bf16)
            total[at, :] = coarse
            if s == 0:
                total[pl.ds(pl.multiple_of(rows + at.start, tile), tile), :] = coarse
            return carry + jnp.sum((value * value).reshape(tile // 8, 8, cols), axis=0)

        return tiles(s, step, carry)

    def low_near():
        low.arrived(0, 0)
        low.start(1, 1)

    def low_mate():
        low.start(2, 0)
        low.start(2, 1)

    def low_rest():
        low.third()
        low.fourth()

    ahead = {7: [low_mate]}
    after = {1: [top.second, low_near], 5: [top.third, top.fourth], 7: [low_rest]}
    start_y(0)
    start_y(1)
    sums = jnp.zeros((8, cols), f32)
    for i in range(8):
        k, s = divmod(i, 2)
        y_copies[i].wait_recv()
        if i + 2 < 8:
            start_y(i + 2)
        for job in ahead.get(i, ()):
            job()
        if k < 2:
            start_z(k, s, None)
        elif k == 2:
            start_z(k, s, 0)
        else:
            sums = close_total(s, sums)
        for job in after.get(i, ()):
            job()
    part = sums[:, :128]
    for c in range(1, cols // 128):
        part = part + sums[:, c * 128 : (c + 1) * 128]
    own_sq[...] = part
    sq_copies = [remote(own_sq, in_sq.at[k], sq_s.at[k], sq_r.at[k], lax.rem(me + 1 + k, n)) for k in range(n - 1)]
    for copy in sq_copies:
        copy.start()

    def product_strip(device):
        at = pl.ds(pl.multiple_of(device * strip, strip), strip)
        right = pl.ds(pl.multiple_of(device * strip, strip), wide)
        return lax.dot_general(total[at, :], total[right, :], (((1,), (1,)), ((), ())), preferred_element_type=f32)

    qy_copies = [remote(strip_y.at[k], got_y.at[k], q_s.at[k], q_r.at[k], flip(me, MATE)) for k in range(4)]
    qz_copies = [remote(strip_z.at[k], got_z.at[k], q_s.at[4 + k], q_r.at[4 + k], flip(me, FAR if k == 2 else NEAR))
                 for k in range(3)]

    def strip_start(k):
        strip_y[k] = product_strip(flip(me, HOPS[k] + MATE)).astype(bf16)
        qy_copies[k].start()

    def strip_pass(k):
        value = product_strip(flip(me, HOPS[k]))
        qy_copies[k].wait_recv()
        value = value + got_y[k].astype(f32)
        if k == 2:
            qz_copies[0].wait_recv()
            value = value + got_z[0].astype(f32)
        strip_z[k] = value.astype(bf16)
        qz_copies[k].start()

    for k in range(4):
        strip_start(k)
    value = own_sq[...]
    for k, copy in enumerate(sq_copies):
        copy.wait()
        value = value + in_sq[k]
    lane_sq[...] = value
    lane_copies = [remote(lane_sq, in_lane.at[k], lane_s.at[k], lane_r.at[k], lax.rem(lane + 1 + k, lanes), "tp")
                   for k in range(lanes - 1)]
    for copy in lane_copies:
        copy.start()
    strip_pass(0)
    for k, copy in enumerate(lane_copies):
        copy.wait()
        value = value + in_lane[k]
    squares = jnp.sum(value, keepdims=True)
    ratio = jnp.minimum(1.0, jnp.sqrt(float(D * KVW) / (squares + 1e-06)))
    strip_pass(1)

    top.last()
    low.last()
    for copy in states[1:]:
        copy.wait()
    part = rows // PARTS

    def rotate(i, carry):
        at = pl.ds(pl.multiple_of(i * part, part), part)
        rotated = lax.dot_general(whole[:, at], total[:rows, :], (((0,), (0,)), ((), ())), preferred_element_type=f32) * ratio
        first = 0.9 * moment_new[at, :] + 0.1 * rotated
        square = 0.95 * second_new[at, :] + 0.05 * rotated * rotated
        moment_new[at, :] = first
        second_new[at, :] = square
        update[at, :] = (first / (jnp.sqrt(square) + 1e-08)).astype(bf16)
        return carry

    lax.fori_loop(0, PARTS, rotate, 0)
    strip_pass(2)
    def weight_window(i):
        def window(device):
            return weights.at[pl.ds(i * part, part), pl.ds(pl.multiple_of(device * cols, 128), cols)]
        return window

    mine = pl.ds(pl.multiple_of(me * cols, 128), cols)
    out = [Gather(me, PLAN[i], weight_window(i), w_s.at[i], w_r.at[i])
           for i in range(PARTS)]
    for i in range(PARTS):
        at = pl.ds(i * part, part)
        delta = jnp.dot(whole[at, :], update[...], preferred_element_type=f32)
        value = master_new[at, :]
        value = value - 0.01 * (delta + 0.1 * value)
        master_new[at, :] = value
        weights[at, mine] = value.astype(bf16)
        out[i].mate()
        if i < READY:
            out[i].line()
    value = product_strip(me)
    qy_copies[3].wait_recv()
    qz_copies[1].wait_recv()
    value = value + got_y[3].astype(f32) + got_z[1].astype(f32)
    qz_copies[2].wait_recv()
    value = value + got_z[2].astype(f32)
    crossing = []
    for k in range(1, HALF - 1):
        block_out[k - 1] = value[:, k * strip : (k + 1) * strip].astype(bf16)
        crossing.append(remote(block_out.at[k - 1], block_in.at[k - 1], x_s.at[k - 1], x_r.at[k - 1], lax.rem(me + k, n)))
        crossing[-1].start()

    def renew(offset, block):
        at = pl.ds(pl.multiple_of(lax.rem(me + offset, n) * strip, strip), strip)
        stats_new[:, at] = 0.9 * stats_new[:, at] + 0.1 / KVW * (block * (ratio * ratio))

    for k in range(HALF):
        renew(k, value[:, k * strip : (k + 1) * strip])
    for k in range(1, HALF - 1):
        crossing[k - 1].wait_recv()
        renew(n - k, block_in[k - 1].astype(f32).T)
    fresh = stats_new[...]
    coarse = fresh.astype(bf16)
    value = (jnp.dot(coarse, whole[...], preferred_element_type=f32)
             + jnp.dot((fresh - coarse.astype(f32)).astype(bf16), whole[...], preferred_element_type=f32))
    power[...] = value
    every[here, :] = value.astype(bf16)

    def power_window(device):
        return every.at[pl.ds(pl.multiple_of(device * strip, strip), strip)]

    spread = Gather(me, LATE, power_window, p_s, p_r)
    spread.first()
    spread.second()
    spread.third()
    spread.fourth()
    out[1].line()
    out[2].line()
    out[1].second()
    out[0].second()
    out[1].third()
    out[3].line()
    spread.last()

    def squares_of(i, carry):
        value = every[pl.ds(pl.multiple_of(i * 128, 128), 128), :].astype(f32)
        return carry + jnp.sum((value * value).reshape(16, 8, rows), axis=0)

    total_sq = jnp.sum(lax.fori_loop(0, rows // 128, squares_of, jnp.zeros((8, rows), f32)), keepdims=True)
    norm = 1.0 / jnp.sqrt(total_sq + 1e-06)
    block = 512

    def make_gram(at):
        value = lax.dot_general(every[:, at], every[...], (((0,), (0,)), ((), ())), preferred_element_type=f32)
        value = value * (norm * norm)
        gram[at, :] = value
        gram_low[at, :] = value.astype(bf16)

    def make_bend(at):
        value = poly_second * gram[at, :] + poly_third * mm(gram_low[at, :], gram_low[...])
        bend[at, :] = value.astype(bf16)

    def make_once(at):
        value = poly_first * gram[at, :] + mm(bend[at, :], gram_low[...])
        gram[at, :] = value
        once[at, :] = value.astype(bf16)

    def make_second(at):
        value = poly_first * gram[at, :] + mm(bend[at, :], once[...])
        gram_low[at, :] = value.astype(bf16)

    def finish():
        current = power[...] * norm
        current = poly_first * current + mm(current, bend[...])
        product = mm(current, gram_low[...])
        refreshed[...] = poly_first * current + poly_second * product + poly_third * mm(product, gram_low[...])

    halves = [pl.ds(start, block) for start in range(0, rows, block)]
    work = [functools.partial(step, at) for step in (make_gram, make_bend, make_once, make_second) for at in halves]
    work.append(finish)
    work.pop(0)()
    out[2].second()
    work.pop(0)()
    out[1].fourth()
    out[2].third()
    work.pop(0)()
    out[3].second()
    work.pop(0)()
    out[0].third()
    out[2].fourth()
    work.pop(0)()
    out[3].third()
    work.pop(0)()
    out[3].fourth()
    work.pop(0)()
    out[0].fourth()
    for step in work:
        step()
    for gather in out:
        gather.last()
    for copy in y_copies + z_copies + qy_copies + qz_copies + crossing:
        copy.wait_send()
    for gather in [top, low, spread] + out:
        gather.close()


def hand_over(*refs):
    count = len(refs) // 2
    copies = [pltpu.make_async_copy(refs[i], refs[count + i], refs[-1].at[i]) for i in range(count)]
    for copy in copies:
        copy.start()
    for copy in copies:
        copy.wait()


def whole_step(grads, master, moment, second, stats, basis, n, lanes):
    unused, micro, rows, width = grads.shape
    cols = width // n
    strip = basis.shape[1]
    dma = pltpu.SemaphoreType.DMA
    vmem = pltpu.VMEM
    slab = (rows, cols)
    row = (strip, rows)
    part = (strip, HALF * strip)
    low = vmem((rows, rows), bf16)
    small = vmem((8, 128), f32)
    others = max(lanes - 1, 1)
    block = pl.BlockSpec(memory_space=pltpu.VMEM)
    far_block = pl.BlockSpec(memory_space=pltpu.HBM)
    f32_slab = jax.ShapeDtypeStruct(slab, f32)
    f32_row = jax.ShapeDtypeStruct(row, f32)
    outs = pl.pallas_call(
        functools.partial(whole_kernel, n, lanes),
        out_shape=(jax.ShapeDtypeStruct((rows, width), bf16), f32_slab, f32_slab, f32_slab, f32_row, f32_row),
        in_specs=[far_block] * 6,
        out_specs=(block,) * 6,
        scratch_shapes=[
            vmem((n, micro) + slab, bf16), vmem((4,) + slab, bf16), vmem((4,) + slab, bf16),
            vmem((3,) + slab, bf16), vmem((3,) + slab, bf16), low, vmem((rows + rows // 2, cols), bf16), vmem(slab, bf16),
            vmem((4,) + part, bf16), vmem((4,) + part, bf16), vmem((3,) + part, bf16), vmem((3,) + part, bf16),
            vmem((HALF - 2, strip, strip), bf16), vmem((HALF - 2, strip, strip), bf16),
            low, vmem(row, f32), vmem((rows, rows), f32), low, low, low,
            small, vmem((n - 1, 8, 128), f32), small, vmem((others, 8, 128), f32),
            dma((n + 5,)), dma((8,)), dma((8,)), dma((6,)), dma((6,)), dma((7,)), dma((7,)),
            dma((n - 1,)), dma((n - 1,)), dma((others,)), dma((others,)),
            dma((2, 7)), dma((2, 7)), dma((7,)), dma((7,)), dma((PARTS, 7)), dma((PARTS, 7)), dma((HALF - 2,)), dma((HALF - 2,)),
        ],
        compiler_params=pltpu.CompilerParams(collective_id=0, has_side_effects=True, vmem_limit_bytes=VMEM_WHOLE),
    )(*(pltpu.with_memory_space_constraint(value, pltpu.HBM) for value in (
        grads, basis[0], stats[0], master, moment, second)))
    weights, master_new, moment_new, second_new, stats_new, current = pl.pallas_call(
        hand_over,
        out_shape=tuple(jax.ShapeDtypeStruct(value.shape, value.dtype) for value in outs),
        in_specs=[block] * len(outs),
        out_specs=(far_block,) * len(outs),
        scratch_shapes=[dma((len(outs),))],
        compiler_params=pltpu.CompilerParams(vmem_limit_bytes=16 * 1024 * 1024),
    )(*outs)
    return (weights, master_new, moment_new, second_new, stats_new[None], current[None])


def plain_grads(grads, n, lanes):
    rows = grads.shape[2]
    local = jnp.sum(grads.astype(f32), axis=(0, 1)).astype(bf16)
    pieces = lax.all_to_all(local, "fsdp", split_axis=1, concat_axis=0, tiled=True)
    summed = jnp.sum(pieces.reshape(n, rows, -1).astype(f32), axis=0)
    squares = lax.psum(jnp.sum(summed * summed), ("fsdp", "tp"))
    return summed.astype(bf16), squares


def body(n, lanes, grads, master, moment, second, stats, basis):
    rows, cols = master.shape
    if n == 8 and cols % 128 == 0 and rows % (16 * PARTS) == 0 and basis.shape[1] % 128 == 0:
        return whole_step(grads, master, moment, second, stats, basis, n, lanes)
    own_rows = basis[0]
    stat_rows = stats[0]
    whole = lax.all_gather(own_rows.astype(bf16), "fsdp", axis=0, tiled=True)
    total, squares = plain_grads(grads, n, lanes)
    ratio = jnp.minimum(1.0, jnp.sqrt(float(D * KVW) / (squares + 1e-06)))
    rotated = mm(whole.T, total) * ratio
    moment_new = 0.9 * moment + 0.1 * rotated
    second_new = 0.95 * second + 0.05 * rotated * rotated
    update = moment_new / (jnp.sqrt(second_new) + 1e-08)
    delta = mm(whole, update)
    master_new = master - 0.01 * (delta + 0.1 * master)
    outer = sum_outer(total, n) * (ratio * ratio)
    stats_new = 0.9 * stat_rows + 0.1 / KVW * outer
    top = stats_new.astype(bf16)
    power = mm(top, whole) + mm(stats_new - top.astype(f32), whole)
    weights = lax.all_gather(master_new.astype(bf16), "fsdp", axis=1, tiled=True)
    every = gather_rows(power.astype(bf16), n, 2)
    raw = mm(every.T, every)
    norm = 1.0 / jnp.sqrt(jnp.sum(jnp.square(every.astype(f32))) + 1e-06)
    gram = raw * (norm * norm)
    current = power * norm
    bend = poly_second * gram + poly_third * mm(gram, gram)
    current = poly_first * current + mm(current, bend)
    once = poly_first * gram + mm(bend, gram)
    gram = poly_first * once + mm(bend, once)
    product = mm(current, gram)
    current = poly_first * current + poly_second * product + poly_third * mm(product, gram)
    return (weights, master_new, moment_new, second_new, stats_new[None], current[None])


def solution(mesh):
    in_specs = (
        P("fsdp", None, "tp", None),
        P("tp", "fsdp"),
        P("tp", "fsdp"),
        P("tp", "fsdp"),
        P("tp", "fsdp", None),
        P("tp", "fsdp", None),
    )
    out_specs = (
        P("tp", None),
        P("tp", "fsdp"),
        P("tp", "fsdp"),
        P("tp", "fsdp"),
        P("tp", "fsdp", None),
        P("tp", "fsdp", None),
    )
    step = functools.partial(body, mesh.shape["fsdp"], mesh.shape["tp"])
    return jax.shard_map(step, mesh=mesh, in_specs=in_specs, out_specs=out_specs, check_vma=False)
```

```python
import functools

import jax
import jax.numpy as jnp
from jax import lax
from jax.experimental import pallas as pl
from jax.experimental.pallas import tpu as pltpu
from jax.sharding import PartitionSpec as P

D = 4096
KVW = 2048

poly_first = 3.4445
poly_second = -4.775
poly_third = 2.0315
bf16 = jnp.bfloat16
f32 = jnp.float32
MESH = pl.DeviceIdType.MESH
VMEM_BYTES = 40 * 1024 * 1024


def mm(a, b):
    return jnp.dot(a.astype(bf16), b.astype(bf16), preferred_element_type=f32)


def greet(n, tp_peers):
    me = lax.axis_index("fsdp")
    barrier = pltpu.get_barrier_semaphore()
    for step in range(1, n):
        pl.semaphore_signal(barrier, inc=1, device_id={"fsdp": lax.rem(me + step, n)}, device_id_type=MESH)
    if tp_peers > 1:
        lane = lax.axis_index("tp")
        for step in range(1, tp_peers):
            pl.semaphore_signal(barrier, inc=1, device_id={"tp": lax.rem(lane + step, tp_peers)}, device_id_type=MESH)
    pl.semaphore_wait(barrier, n - 1 + tp_peers - 1)


def remote(src, dst, send_sem, recv_sem, target, axis="fsdp"):
    return pltpu.make_async_remote_copy(
        src_ref=src, dst_ref=dst, send_sem=send_sem, recv_sem=recv_sem,
        device_id={axis: target}, device_id_type=MESH,
    )


def exchange(n, produce, finish, out1, in1, out2, in2, s1, r1, s2, r2, beside=None):
    half = n // 2
    me = lax.axis_index("fsdp")
    side = lax.rem(me, 2)
    pair = me // 2
    mate = me + 1 - 2 * side
    groups = [lax.rem(pair + 1 + k, half) for k in range(half)]
    first = [remote(out1.at[k], in1.at[k], s1.at[k], r1.at[k], mate) for k in range(half)]
    second = [remote(out2.at[k], in2.at[k], s2.at[k], r2.at[k], 2 * groups[k] + side) for k in range(half - 1)]

    def start(k):
        produce(2 * groups[k] + 1 - side, 2 * k, None, out1.at[k])
        first[k].start()

    for k in range(min(2, half)):
        start(k)
    for k in range(half):
        first[k].wait_recv()
        if k + 2 < half:
            start(k + 2)
        if k < half - 1:
            produce(2 * groups[k] + side, 2 * k + 1, in1.at[k], out2.at[k])
            second[k].start()
        if beside is not None:
            beside(k)
    for k in range(half - 1):
        second[k].wait_recv()
    finish(me, 2 * half - 1, in1.at[half - 1], in2)
    for k in range(half):
        first[k].wait_send()
    for k in range(half - 1):
        second[k].wait_send()


def outer_kernel(n, total, outer, out1, in1, out2, in2, s1, r1, s2, r2):
    half = n // 2
    strip = outer.shape[0]
    greet(n, 1)

    def local(chunk):
        at = pl.ds(pl.multiple_of(chunk * strip, strip), strip)
        return lax.dot_general(total[at, :], total[...], (((1,), (1,)), ((), ())), preferred_element_type=f32)

    def produce(chunk, slot, add, out):
        value = local(chunk)
        if add is not None:
            value = value + add[...].astype(f32)
        out[...] = value.astype(bf16)

    def finish(chunk, slot, add, others):
        value = local(chunk) + add[...].astype(f32)
        for k in range(half - 1):
            value = value + others[k].astype(f32)
        outer[...] = value

    exchange(n, produce, finish, out1, in1, out2, in2, s1, r1, s2, r2)


def sum_outer(total, n):
    rows = total.shape[0]
    strip = rows // n
    half = n // 2
    small = max(half - 1, 1)
    dma = pltpu.SemaphoreType.DMA
    piece = pltpu.VMEM((half, strip, rows), bf16)
    other = pltpu.VMEM((small, strip, rows), bf16)
    return pl.pallas_call(
        functools.partial(outer_kernel, n),
        out_shape=jax.ShapeDtypeStruct((strip, rows), f32),
        in_specs=[pl.BlockSpec(memory_space=pltpu.VMEM)],
        out_specs=pl.BlockSpec(memory_space=pltpu.VMEM),
        scratch_shapes=[piece, piece, other, other, dma((half,)), dma((half,)), dma((small,)), dma((small,))],
        compiler_params=pltpu.CompilerParams(collective_id=1, has_side_effects=True, vmem_limit_bytes=VMEM_BYTES),
    )(total)


def gather_kernel(n, own, every, s1, r1, s2, r2):
    half = n // 2
    me = lax.axis_index("fsdp")
    side = lax.rem(me, 2)
    pair = me // 2
    mate = me + 1 - 2 * side
    greet(n, 1)
    across = [remote(own, every.at[me], s2.at[k], r2.at[k], 2 * lax.rem(pair + 1 + k, half) + side)
              for k in range(half - 1)]
    for copy in across:
        copy.start()
    near = [remote(own, every.at[me], s1.at[0], r1.at[0], mate)]
    near[0].start()
    every[me] = own[...]
    for k in range(half - 1):
        across[k].wait_recv()
        source = 2 * lax.rem(pair + half - 1 - k, half) + side
        near.append(remote(every.at[source], every.at[source], s1.at[k + 1], r1.at[k + 1], mate))
        near[-1].start()
    for copy in near:
        copy.wait()
    for copy in across:
        copy.wait_send()


def gather_rows(own, n, key):
    strip, width = own.shape
    half = n // 2
    small = max(half - 1, 1)
    dma = pltpu.SemaphoreType.DMA
    every = pl.pallas_call(
        functools.partial(gather_kernel, n),
        out_shape=jax.ShapeDtypeStruct((n, strip, width), own.dtype),
        in_specs=[pl.BlockSpec(memory_space=pltpu.VMEM)],
        out_specs=pl.BlockSpec(memory_space=pltpu.VMEM),
        scratch_shapes=[dma((half,)), dma((half,)), dma((small,)), dma((small,))],
        compiler_params=pltpu.CompilerParams(collective_id=key, has_side_effects=True, vmem_limit_bytes=VMEM_BYTES),
    )(own)
    return every.reshape(n * strip, width)


MATE, NEAR, FAR = 1, 2, 4
LATE = (FAR, NEAR, MATE)
MIDDLE = (FAR, MATE, NEAR)
EARLY = (MATE, FAR, NEAR)
PARTS = 4
READY = 1
VMEM_WHOLE = 41 * 1024 * 1024
PLAN = (MIDDLE, LATE, LATE, LATE)
HALF = 5
ALONG = 80
HOPS = (FAR + NEAR, NEAR, FAR, 0)


def flip(device, mask):
    for bit in (MATE, NEAR, FAR):
        if mask & bit:
            device = device + bit - 2 * bit * lax.rem(device // bit, 2)
    return device


class Gather:
    def __init__(self, me, order, window, sends, recvs):
        self.me, self.order, self.window, self.sends, self.recvs = me, order, window, sends, recvs
        self.sent = []

    def copy(self, stage, sub):
        mask = sum(bit for i, bit in enumerate(self.order) if sub >> i & 1)
        place = self.window(flip(self.me, mask))
        index = 2 ** stage - 1 + sub
        return remote(place, place, self.sends.at[index], self.recvs.at[index], flip(self.me, self.order[stage]))

    def start(self, stage, sub):
        copy = self.copy(stage, sub)
        copy.start()
        self.sent.append(copy)

    def arrived(self, stage, sub):
        self.copy(stage, sub).wait_recv()

    def mate(self):
        self.start(self.order.index(MATE), 0)

    def line(self):
        for bit in (FAR, NEAR):
            self.start(self.order.index(bit), 0)

    def first(self):
        for stage in range(3):
            self.start(stage, 0)

    def second(self):
        self.arrived(0, 0)
        self.start(1, 1)
        self.start(2, 1)

    def third(self):
        self.arrived(1, 0)
        self.start(2, 2)

    def fourth(self):
        self.arrived(1, 1)
        self.start(2, 3)

    def last(self):
        for sub in range(4):
            self.arrived(2, sub)

    def close(self):
        for copy in self.sent:
            copy.wait_send()


def whole_kernel(n, lanes, grads, basis, stats, master, moment, second,
                 weights, master_new, moment_new, second_new, stats_new, refreshed,
                 held, out_y, in_y, out_z, in_z, whole, total, update,
                 strip_y, got_y, strip_z, got_z, block_out, block_in, every, power, gram, gram_low, bend, once,
                 own_sq, in_sq, lane_sq, in_lane,
                 loads, y_s, y_r, z_s, z_r, q_s, q_r, sq_s, sq_r, lane_s, lane_r, b_s, b_r, p_s, p_r, w_s, w_r, x_s, x_r):
    rows, cols = moment_new.shape
    strip = stats.shape[0]
    wide = HALF * strip
    micro = held.shape[1]
    tile = 128
    piece = rows // 2
    me = lax.axis_index("fsdp")
    lane = lax.axis_index("tp")

    copies = []
    for k, mask in enumerate(HOPS):
        for which in (MATE, 0):
            start = pl.multiple_of(flip(me, mask + which) * cols, 128)
            slot = len(copies)
            copies.append(pltpu.make_async_copy(grads.at[0, :, :, pl.ds(start, cols)], held.at[slot], loads.at[slot]))
    states = [pltpu.make_async_copy(source, place, loads.at[n + i]) for i, (source, place) in enumerate(
        ((basis, refreshed), (moment, moment_new), (second, second_new), (master, master_new), (stats, stats_new)))]
    for copy in copies[:1] + states[:1] + copies[1:] + states[1:]:
        copy.start()
    greet(n, lanes)

    here = pl.ds(pl.multiple_of(me * strip, strip), strip)
    states[0].wait()
    whole[here, :] = refreshed[...].astype(bf16)

    def basis_window(shift, count):
        def window(device):
            return whole.at[pl.ds(pl.multiple_of(device * strip + shift, 16), count)]
        return window

    low = Gather(me, LATE, basis_window(0, strip - ALONG), b_s.at[0], b_r.at[0])
    top = Gather(me, EARLY, basis_window(strip - ALONG, ALONG), b_s.at[1], b_r.at[1])
    top.first()
    low.start(0, 0)
    low.start(1, 0)

    def local(slot, at):
        value = held[slot, 0, at, :].astype(f32)
        for index in range(1, micro):
            value = value + held[slot, index, at, :].astype(f32)
        return value

    def tiles(s, step, carry=0):
        def run(i, carry):
            return step(pl.ds(pl.multiple_of(s * piece + i * tile, tile), tile), carry)
        return lax.fori_loop(0, piece // tile, run, carry)

    def span(s):
        return pl.ds(s * piece, piece)

    y_copies = [remote(out_y.at[i // 2, span(i % 2)], in_y.at[i // 2, span(i % 2)], y_s.at[i], y_r.at[i], flip(me, MATE))
                for i in range(8)]
    z_copies = [remote(out_z.at[i // 2, span(i % 2)], in_z.at[i // 2, span(i % 2)], z_s.at[i], z_r.at[i],
                       flip(me, NEAR if i < 4 else FAR)) for i in range(6)]

    def start_y(i):
        k, s = divmod(i, 2)
        if s == 0:
            copies[2 * k].wait()

        def step(at, carry):
            out_y[k, at, :] = local(2 * k, at).astype(bf16)
            return carry

        tiles(s, step)
        y_copies[i].start()

    def start_z(k, s, extra):
        if s == 0:
            copies[2 * k + 1].wait()
        if extra is not None:
            z_copies[2 * extra + s].wait_recv()

        def step(at, carry):
            value = local(2 * k + 1, at) + in_y[k, at, :].astype(f32)
            if extra is not None:
                value = value + in_z[extra, at, :].astype(f32)
            out_z[k, at, :] = value.astype(bf16)
            return carry

        tiles(s, step)
        z_copies[2 * k + s].start()

    def close_total(s, carry):
        if s == 0:
            copies[7].wait()
        z_copies[2 + s].wait_recv()
        z_copies[4 + s].wait_recv()

        def step(at, carry):
            value = local(7, at) + in_y[3, at, :].astype(f32) + in_z[1, at, :].astype(f32) + in_z[2, at, :].astype(f32)
            coarse = value.astype(bf16)
            total[at, :] = coarse
            if s == 0:
                total[pl.ds(pl.multiple_of(rows + at.start, tile), tile), :] = coarse
            return carry + jnp.sum((value * value).reshape(tile // 8, 8, cols), axis=0)

        return tiles(s, step, carry)

    def low_near():
        low.arrived(0, 0)
        low.start(1, 1)

    def low_mate():
        low.start(2, 0)
        low.start(2, 1)

    def low_rest():
        low.third()
        low.fourth()

    ahead = {7: [low_mate]}
    after = {1: [top.second, low_near], 5: [top.third], 6: [top.fourth], 7: [low_rest]}
    start_y(0)
    start_y(1)
    sums = jnp.zeros((8, cols), f32)
    for i in range(8):
        k, s = divmod(i, 2)
        y_copies[i].wait_recv()
        if i + 2 < 8:
            start_y(i + 2)
        for job in ahead.get(i, ()):
            job()
        if k < 2:
            start_z(k, s, None)
        elif k == 2:
            start_z(k, s, 0)
        else:
            sums = close_total(s, sums)
        for job in after.get(i, ()):
            job()
    part = sums[:, :128]
    for c in range(1, cols // 128):
        part = part + sums[:, c * 128 : (c + 1) * 128]
    own_sq[...] = part
    sq_copies = [remote(own_sq, in_sq.at[k], sq_s.at[k], sq_r.at[k], lax.rem(me + 1 + k, n)) for k in range(n - 1)]
    for copy in sq_copies:
        copy.start()

    def product_strip(device):
        at = pl.ds(pl.multiple_of(device * strip, strip), strip)
        right = pl.ds(pl.multiple_of(device * strip, strip), wide)
        return lax.dot_general(total[at, :], total[right, :], (((1,), (1,)), ((), ())), preferred_element_type=f32)

    qy_copies = [remote(strip_y.at[k], got_y.at[k], q_s.at[k], q_r.at[k], flip(me, MATE)) for k in range(4)]
    qz_copies = [remote(strip_z.at[k], got_z.at[k], q_s.at[4 + k], q_r.at[4 + k], flip(me, FAR if k == 2 else NEAR))
                 for k in range(3)]

    def strip_start(k):
        strip_y[k] = product_strip(flip(me, HOPS[k] + MATE)).astype(bf16)
        qy_copies[k].start()

    def strip_pass(k):
        value = product_strip(flip(me, HOPS[k]))
        qy_copies[k].wait_recv()
        value = value + got_y[k].astype(f32)
        if k == 2:
            qz_copies[0].wait_recv()
            value = value + got_z[0].astype(f32)
        strip_z[k] = value.astype(bf16)
        qz_copies[k].start()

    for k in range(4):
        strip_start(k)
    value = own_sq[...]
    for k, copy in enumerate(sq_copies):
        copy.wait()
        value = value + in_sq[k]
    lane_sq[...] = value
    lane_copies = [remote(lane_sq, in_lane.at[k], lane_s.at[k], lane_r.at[k], lax.rem(lane + 1 + k, lanes), "tp")
                   for k in range(lanes - 1)]
    for copy in lane_copies:
        copy.start()
    strip_pass(0)
    for k, copy in enumerate(lane_copies):
        copy.wait()
        value = value + in_lane[k]
    squares = jnp.sum(value, keepdims=True)
    ratio = jnp.minimum(1.0, jnp.sqrt(float(D * KVW) / (squares + 1e-06)))
    strip_pass(1)

    top.last()
    low.last()
    for copy in states[1:]:
        copy.wait()
    part = rows // PARTS

    def rotate(i, carry):
        at = pl.ds(pl.multiple_of(i * part, part), part)
        rotated = lax.dot_general(whole[:, at], total[:rows, :], (((0,), (0,)), ((), ())), preferred_element_type=f32) * ratio
        first = 0.9 * moment_new[at, :] + 0.1 * rotated
        square = 0.95 * second_new[at, :] + 0.05 * rotated * rotated
        moment_new[at, :] = first
        second_new[at, :] = square
        update[at, :] = (first / (jnp.sqrt(square) + 1e-08)).astype(bf16)
        return carry

    lax.fori_loop(0, PARTS, rotate, 0)
    strip_pass(2)
    def weight_window(i):
        def window(device):
            return weights.at[pl.ds(i * part, part), pl.ds(pl.multiple_of(device * cols, 128), cols)]
        return window

    mine = pl.ds(pl.multiple_of(me * cols, 128), cols)
    out = [Gather(me, PLAN[i], weight_window(i), w_s.at[i], w_r.at[i])
           for i in range(PARTS)]
    for i in range(PARTS):
        at = pl.ds(i * part, part)
        delta = jnp.dot(whole[at, :], update[...], preferred_element_type=f32)
        value = master_new[at, :]
        value = value - 0.01 * (delta + 0.1 * value)
        master_new[at, :] = value
        weights[at, mine] = value.astype(bf16)
        out[i].mate()
        if i < READY:
            out[i].line()
    value = product_strip(me)
    qy_copies[3].wait_recv()
    qz_copies[1].wait_recv()
    value = value + got_y[3].astype(f32) + got_z[1].astype(f32)
    qz_copies[2].wait_recv()
    value = value + got_z[2].astype(f32)
    crossing = []
    for k in range(1, HALF - 1):
        block_out[k - 1] = value[:, k * strip : (k + 1) * strip].astype(bf16)
        crossing.append(remote(block_out.at[k - 1], block_in.at[k - 1], x_s.at[k - 1], x_r.at[k - 1], lax.rem(me + k, n)))
        crossing[-1].start()

    def renew(offset, block):
        at = pl.ds(pl.multiple_of(lax.rem(me + offset, n) * strip, strip), strip)
        stats_new[:, at] = 0.9 * stats_new[:, at] + 0.1 / KVW * (block * (ratio * ratio))

    for k in range(HALF):
        renew(k, value[:, k * strip : (k + 1) * strip])
    for k in range(1, HALF - 1):
        crossing[k - 1].wait_recv()
        renew(n - k, block_in[k - 1].astype(f32).T)
    fresh = stats_new[...]
    coarse = fresh.astype(bf16)
    value = (jnp.dot(coarse, whole[...], preferred_element_type=f32)
             + jnp.dot((fresh - coarse.astype(f32)).astype(bf16), whole[...], preferred_element_type=f32))
    power[...] = value
    every[here, :] = value.astype(bf16)

    def power_window(device):
        return every.at[pl.ds(pl.multiple_of(device * strip, strip), strip)]

    spread = Gather(me, LATE, power_window, p_s, p_r)
    spread.first()
    spread.second()
    spread.third()
    spread.fourth()
    out[1].line()
    out[2].line()
    out[1].second()
    out[0].second()
    out[1].third()
    out[3].line()
    spread.last()

    def squares_of(i, carry):
        value = every[pl.ds(pl.multiple_of(i * 128, 128), 128), :].astype(f32)
        return carry + jnp.sum((value * value).reshape(16, 8, rows), axis=0)

    total_sq = jnp.sum(lax.fori_loop(0, rows // 128, squares_of, jnp.zeros((8, rows), f32)), keepdims=True)
    norm = 1.0 / jnp.sqrt(total_sq + 1e-06)
    block = 512

    def make_gram(at):
        value = lax.dot_general(every[:, at], every[...], (((0,), (0,)), ((), ())), preferred_element_type=f32)
        value = value * (norm * norm)
        gram[at, :] = value
        gram_low[at, :] = value.astype(bf16)

    def make_bend(at):
        value = poly_second * gram[at, :] + poly_third * mm(gram_low[at, :], gram_low[...])
        bend[at, :] = value.astype(bf16)

    def make_once(at):
        value = poly_first * gram[at, :] + mm(bend[at, :], gram_low[...])
        gram[at, :] = value
        once[at, :] = value.astype(bf16)

    def make_second(at):
        value = poly_first * gram[at, :] + mm(bend[at, :], once[...])
        gram_low[at, :] = value.astype(bf16)

    def finish():
        current = power[...] * norm
        current = poly_first * current + mm(current, bend[...])
        product = mm(current, gram_low[...])
        refreshed[...] = poly_first * current + poly_second * product + poly_third * mm(product, gram_low[...])

    halves = [pl.ds(start, block) for start in range(0, rows, block)]
    work = [functools.partial(step, at) for step in (make_gram, make_bend, make_once, make_second) for at in halves]
    work.append(finish)
    work.pop(0)()
    out[2].second()
    work.pop(0)()
    out[1].fourth()
    out[2].third()
    work.pop(0)()
    out[3].second()
    work.pop(0)()
    out[0].third()
    out[2].fourth()
    work.pop(0)()
    out[3].third()
    work.pop(0)()
    out[3].fourth()
    work.pop(0)()
    out[0].fourth()
    for step in work:
        step()
    for gather in out:
        gather.last()
    for copy in y_copies + z_copies + qy_copies + qz_copies + crossing:
        copy.wait_send()
    for gather in [top, low, spread] + out:
        gather.close()


def hand_over(*refs):
    count = len(refs) // 2
    copies = [pltpu.make_async_copy(refs[i], refs[count + i], refs[-1].at[i]) for i in range(count)]
    for copy in copies:
        copy.start()
    for copy in copies:
        copy.wait()


def whole_step(grads, master, moment, second, stats, basis, n, lanes):
    unused, micro, rows, width = grads.shape
    cols = width // n
    strip = basis.shape[1]
    dma = pltpu.SemaphoreType.DMA
    vmem = pltpu.VMEM
    slab = (rows, cols)
    row = (strip, rows)
    part = (strip, HALF * strip)
    low = vmem((rows, rows), bf16)
    small = vmem((8, 128), f32)
    others = max(lanes - 1, 1)
    block = pl.BlockSpec(memory_space=pltpu.VMEM)
    far_block = pl.BlockSpec(memory_space=pltpu.HBM)
    f32_slab = jax.ShapeDtypeStruct(slab, f32)
    f32_row = jax.ShapeDtypeStruct(row, f32)
    outs = pl.pallas_call(
        functools.partial(whole_kernel, n, lanes),
        out_shape=(jax.ShapeDtypeStruct((rows, width), bf16), f32_slab, f32_slab, f32_slab, f32_row, f32_row),
        in_specs=[far_block] * 6,
        out_specs=(block,) * 6,
        scratch_shapes=[
            vmem((n, micro) + slab, bf16), vmem((4,) + slab, bf16), vmem((4,) + slab, bf16),
            vmem((3,) + slab, bf16), vmem((3,) + slab, bf16), low, vmem((rows + rows // 2, cols), bf16), vmem(slab, bf16),
            vmem((4,) + part, bf16), vmem((4,) + part, bf16), vmem((3,) + part, bf16), vmem((3,) + part, bf16),
            vmem((HALF - 2, strip, strip), bf16), vmem((HALF - 2, strip, strip), bf16),
            low, vmem(row, f32), vmem((rows, rows), f32), low, low, low,
            small, vmem((n - 1, 8, 128), f32), small, vmem((others, 8, 128), f32),
            dma((n + 5,)), dma((8,)), dma((8,)), dma((6,)), dma((6,)), dma((7,)), dma((7,)),
            dma((n - 1,)), dma((n - 1,)), dma((others,)), dma((others,)),
            dma((2, 7)), dma((2, 7)), dma((7,)), dma((7,)), dma((PARTS, 7)), dma((PARTS, 7)), dma((HALF - 2,)), dma((HALF - 2,)),
        ],
        compiler_params=pltpu.CompilerParams(collective_id=0, has_side_effects=True, vmem_limit_bytes=VMEM_WHOLE),
    )(*(pltpu.with_memory_space_constraint(value, pltpu.HBM) for value in (
        grads, basis[0], stats[0], master, moment, second)))
    weights, master_new, moment_new, second_new, stats_new, current = pl.pallas_call(
        hand_over,
        out_shape=tuple(jax.ShapeDtypeStruct(value.shape, value.dtype) for value in outs),
        in_specs=[block] * len(outs),
        out_specs=(far_block,) * len(outs),
        scratch_shapes=[dma((len(outs),))],
        compiler_params=pltpu.CompilerParams(vmem_limit_bytes=16 * 1024 * 1024),
    )(*outs)
    return (weights, master_new, moment_new, second_new, stats_new[None], current[None])


def plain_grads(grads, n, lanes):
    rows = grads.shape[2]
    local = jnp.sum(grads.astype(f32), axis=(0, 1)).astype(bf16)
    pieces = lax.all_to_all(local, "fsdp", split_axis=1, concat_axis=0, tiled=True)
    summed = jnp.sum(pieces.reshape(n, rows, -1).astype(f32), axis=0)
    squares = lax.psum(jnp.sum(summed * summed), ("fsdp", "tp"))
    return summed.astype(bf16), squares


def body(n, lanes, grads, master, moment, second, stats, basis):
    rows, cols = master.shape
    if n == 8 and cols % 128 == 0 and rows % (16 * PARTS) == 0 and basis.shape[1] % 128 == 0:
        return whole_step(grads, master, moment, second, stats, basis, n, lanes)
    own_rows = basis[0]
    stat_rows = stats[0]
    whole = lax.all_gather(own_rows.astype(bf16), "fsdp", axis=0, tiled=True)
    total, squares = plain_grads(grads, n, lanes)
    ratio = jnp.minimum(1.0, jnp.sqrt(float(D * KVW) / (squares + 1e-06)))
    rotated = mm(whole.T, total) * ratio
    moment_new = 0.9 * moment + 0.1 * rotated
    second_new = 0.95 * second + 0.05 * rotated * rotated
    update = moment_new / (jnp.sqrt(second_new) + 1e-08)
    delta = mm(whole, update)
    master_new = master - 0.01 * (delta + 0.1 * master)
    outer = sum_outer(total, n) * (ratio * ratio)
    stats_new = 0.9 * stat_rows + 0.1 / KVW * outer
    top = stats_new.astype(bf16)
    power = mm(top, whole) + mm(stats_new - top.astype(f32), whole)
    weights = lax.all_gather(master_new.astype(bf16), "fsdp", axis=1, tiled=True)
    every = gather_rows(power.astype(bf16), n, 2)
    raw = mm(every.T, every)
    norm = 1.0 / jnp.sqrt(jnp.sum(jnp.square(every.astype(f32))) + 1e-06)
    gram = raw * (norm * norm)
    current = power * norm
    bend = poly_second * gram + poly_third * mm(gram, gram)
    current = poly_first * current + mm(current, bend)
    once = poly_first * gram + mm(bend, gram)
    gram = poly_first * once + mm(bend, once)
    product = mm(current, gram)
    current = poly_first * current + poly_second * product + poly_third * mm(product, gram)
    return (weights, master_new, moment_new, second_new, stats_new[None], current[None])


def solution(mesh):
    in_specs = (
        P("fsdp", None, "tp", None),
        P("tp", "fsdp"),
        P("tp", "fsdp"),
        P("tp", "fsdp"),
        P("tp", "fsdp", None),
        P("tp", "fsdp", None),
    )
    out_specs = (
        P("tp", None),
        P("tp", "fsdp"),
        P("tp", "fsdp"),
        P("tp", "fsdp"),
        P("tp", "fsdp", None),
        P("tp", "fsdp", None),
    )
    step = functools.partial(body, mesh.shape["fsdp"], mesh.shape["tp"])
    return jax.shard_map(step, mesh=mesh, in_specs=in_specs, out_specs=out_specs, check_vma=False)
```
